32 devices in a mesh: dp: 4 (over y, x), context: 4 (over z), tensor: 2 (over core).
Axes of the slice: x: 2, y: 2, z: 4, core: 2. Of those that a mesh axis runs over, the one named last changes fastest.
Arguments:
- tokens: bfloat16 [8, 1024, 2048], P('dp', 'context'), may hold values from -6 to 6
- lengths: int32 [8], P('dp'), may hold values from 256 to 1024, as said below
- w_query: bfloat16 [2048, 2048], P(('dp', 'context'), 'tensor'), may hold values from -0.125 to 0.125
- w_key: bfloat16 [2048, 2048], P(('dp', 'context'), 'tensor'), may hold values from -0.125 to 0.125
- w_value: bfloat16 [2048, 2048], P(('dp', 'context'), 'tensor'), may hold values from -0.125 to 0.125
- w_out: bfloat16 [2048, 2048], P('tensor', ('dp', 'context')), may hold values from -1 to 1
- w_gate: bfloat16 [2048, 8192], P(('dp', 'context'), 'tensor'), may hold values from -0.125 to 0.125
- w_up: bfloat16 [2048, 8192], P(('dp', 'context'), 'tensor'), may hold values from -0.125 to 0.125
- w_down: bfloat16 [8192, 2048], P('tensor', ('dp', 'context')), may hold values from -0.0625 to 0.0625
- cotangent: bfloat16 [8, 1024, 2048], P('dp', 'context'), may hold values from -6 to 6
Outputs:
- layer_out: bfloat16 [8, 1024, 2048], P('dp', 'context')
- input_grad: float32 [8, 1024, 2048], P('dp', 'context')
- grad_query: float32 [2048, 2048], P(('dp', 'context'), 'tensor')
- grad_key: float32 [2048, 2048], P(('dp', 'context'), 'tensor')
- grad_value: float32 [2048, 2048], P(('dp', 'context'), 'tensor')
- grad_out: float32 [2048, 2048], P('tensor', ('dp', 'context'))
- grad_gate: float32 [2048, 8192], P(('dp', 'context'), 'tensor')
- grad_up: float32 [2048, 8192], P(('dp', 'context'), 'tensor')
- grad_down: float32 [8192, 2048], P('tensor', ('dp', 'context'))
The draws below stay inside these ranges and needn't reach their ends.
Inputs may be any that keep to these rules, and one draw needn't show every extreme that they name: `lengths`: valid tokens of each slot, counted from its start; in every draw one slot is full and another holds exactly 256.
All inputs are finite; a program needn't handle non-finite values.
Results may differ from the reference program's by a relative error of at most 0.014.
Values may be sent and summed in bfloat16 or wider, within the bound.
A program may use at most 344 MiB of HBM per device.

```python
import math
import jax
import jax.numpy as jnp
from jax import lax

D = 2048
HEADS = 16
HEAD_DIM = 128
FF = 8192
SEQ = 1024
SLOTS = 8


def draw_lengths(key, part):
    key_lengths, key_order = jax.random.split(key)
    lengths_raw = jax.random.randint(key_lengths, (SLOTS,), SEQ // 4, SEQ + 1)
    shuffled = jax.random.permutation(key_order, SLOTS)
    lengths_raw = jnp.where(shuffled == 0, SEQ, lengths_raw)
    lengths_raw = jnp.where(shuffled == 1, SEQ // 4, lengths_raw)
    return lengths_raw.astype(jnp.int32)


def with_spikes(entries, own_key, source, target, blocks, factor):
    owner, partner = [(jnp.arange(entries.shape[dim]) // (entries.shape[dim] // blocks)).reshape([-1 if axis == dim else 1 for axis in range(entries.ndim)]) for dim in (source, target)]
    chosen = jax.random.permutation(own_key, blocks)[partner]
    strong = (owner == chosen) | (owner == (partner + blocks // 2) % blocks)
    return jnp.where(strong, factor * entries, entries)


def block_levels(own_key, dims, cuts, low, high):
    level, own = 1.0, jax.random.fold_in(own_key, 6)
    for axis_at, parts in cuts:
        heights = jnp.exp(jax.random.uniform(jax.random.fold_in(own, axis_at), (parts,), jnp.float32, low / len(cuts), high / len(cuts)))
        level = level * jnp.repeat(heights, dims[axis_at] // parts).reshape([-1 if axis == axis_at else 1 for axis in range(len(dims))])
    return level


def noise(stream_key, extent, scale, reach, pieces=(), kind=jnp.bfloat16):
    entries = scale * jax.random.normal(stream_key, extent, jnp.float32)
    if pieces:
        entries = entries * block_levels(stream_key, extent, pieces, -0.22, 0.18)
    return jnp.clip(entries, -reach, reach).astype(kind)


def bell_draw_with(stream_key, shape, width, limit, pieces, heavy, held_as=jnp.bfloat16):
    result = width * jax.random.normal(stream_key, shape, jnp.float32)
    if pieces:
        result = result * block_levels(stream_key, shape, pieces, -0.22, 0.18)
    return jnp.clip(with_spikes(result, jax.random.fold_in(stream_key, 3), *heavy), -limit, limit).astype(held_as)


def setup_inputs(seed: int = 0) -> dict:
    splits = jax.random.split(jax.random.key(seed), 11)
    tokens = noise(splits[0], (SLOTS, SEQ, D), 1.0, 6.0, ((0, 4), (1, 4)))
    lengths = draw_lengths(jax.random.fold_in(splits[10], 71), 0)
    w_query = noise(splits[2], (D, D), D ** -0.5, 0.125, ((0, 16), (1, 2)))
    w_key = noise(splits[3], (D, D), D ** -0.5, 0.125, ((0, 16), (1, 2)))
    w_value = noise(splits[4], (D, D), D ** -0.5, 0.125, ((0, 16), (1, 2)))
    w_out = noise(splits[5], (D, D), (max(1, D * 16 // SEQ)) ** -0.5, 1.0, ((0, 2), (1, 16)))
    w_gate = noise(splits[6], (D, FF), D ** -0.5, 0.125, ((0, 16), (1, 2)))
    w_up = noise(splits[7], (D, FF), D ** -0.5, 0.125, ((0, 16), (1, 2)))
    w_down = noise(splits[8], (FF, D), FF ** -0.5, 0.0625, ((0, 2), (1, 16)))
    cotangent = bell_draw_with(splits[9], (SLOTS, SEQ, D), 1.0, 6.0, ((0, 4), (1, 4)), (1, 2, 4, 2.0))
    return dict(tokens=tokens, lengths=lengths, w_query=w_query, w_key=w_key, w_value=w_value, w_out=w_out, w_gate=w_gate, w_up=w_up, w_down=w_down, cotangent=cotangent)


@jax.custom_vjp
def low(v):
    return lax.optimization_barrier(v.astype(jnp.bfloat16)).astype(jnp.float32)

@jax.custom_vjp
def low_back(v):
    return v

def low_keep(v):
    return (low(v), None)

def low_pass(kept, grad):
    return (grad,)

def back_keep(v):
    return (v, None)

def back_low(kept, grad):
    return (low(grad),)
low.defvjp(low_keep, low_pass)
low_back.defvjp(back_keep, back_low)

def matmul(left, right):
    return jnp.dot(left, right, precision=lax.Precision.HIGHEST, preferred_element_type=jnp.float32)

def normalize(values):
    centered = values - lax.optimization_barrier(jnp.mean(values, axis=-1, keepdims=True))
    variance = lax.optimization_barrier(jnp.mean(centered * centered, axis=-1, keepdims=True))
    return centered * lax.rsqrt(variance + 1e-05)

def rope_tables(positions, head_dim):
    half_dim = head_dim // 2
    inverse_freq = jnp.exp(-math.log(10000.0) * jnp.arange(half_dim, dtype=jnp.float32) * 2.0 / head_dim)
    angles = positions.astype(jnp.float32)[:, None] * inverse_freq[None, :]
    angles = jnp.concatenate([angles, angles], axis=-1)
    return (jnp.cos(angles)[:, None, :], jnp.sin(angles)[:, None, :])

def rotate(values, cosine, sine):
    half_dim = values.shape[-1] // 2
    turned = jnp.concatenate([-values[..., half_dim:], values[..., :half_dim]], axis=-1)
    return values * cosine + turned * sine

def reference(tokens, lengths, w_query, w_key, w_value, w_out, w_gate, w_up, w_down, cotangent):
    weights = (w_query.astype(jnp.float32), w_key.astype(jnp.float32), w_value.astype(jnp.float32), w_out.astype(jnp.float32), w_gate.astype(jnp.float32), w_up.astype(jnp.float32), w_down.astype(jnp.float32))
    positions = jnp.arange(SEQ, dtype=jnp.int32)
    rope_cos, rope_sin = rope_tables(positions, HEAD_DIM)
    causal = positions[None, :] <= positions[:, None]
    score_scale = 1.0 / math.sqrt(HEAD_DIM)

    def per_slot(gradient_sums, operands):
        slot_tokens, slot_length, slot_cotangent = operands
        valid_rows = (positions < slot_length).astype(jnp.float32)[:, None]
        allowed = causal & (positions < slot_length)[None, :]

        def head_attend(head_operands):
            query_head, key_head, value_head = head_operands
            scores = low_back(jnp.einsum('qd,kd->qk', query_head, key_head, precision=lax.Precision.HIGHEST) * score_scale)
            masked = jnp.where(allowed, scores, -1e+30)
            row_top = lax.optimization_barrier(jnp.max(masked, axis=-1, keepdims=True))
            exponent = jnp.where(allowed, jnp.exp(masked - row_top), 0.0)
            probabilities = low(exponent / lax.optimization_barrier(jnp.sum(exponent, axis=-1, keepdims=True)))
            return matmul(probabilities, value_head)

        def layer_forward(inputs, query_weight, key_weight, value_weight, out_weight, gate_weight, up_weight, down_weight):
            norm_one = low(normalize(inputs))
            query_raw = low_back(matmul(norm_one, query_weight)).reshape(SEQ, HEADS, HEAD_DIM)
            key_raw = low_back(matmul(norm_one, key_weight)).reshape(SEQ, HEADS, HEAD_DIM)
            value_rows = low(low_back(matmul(norm_one, value_weight))).reshape(SEQ, HEADS, HEAD_DIM)
            query_rot = low(rotate(query_raw, rope_cos, rope_sin))
            key_rot = low(rotate(key_raw, rope_cos, rope_sin))
            attended = lax.map(jax.checkpoint(head_attend), (jnp.moveaxis(query_rot, 1, 0), jnp.moveaxis(key_rot, 1, 0), jnp.moveaxis(value_rows, 1, 0)))
            attended = low(low_back(jnp.moveaxis(attended, 0, 1).reshape(SEQ, D)))
            branch = low_back(matmul(attended, out_weight))
            middle = inputs + valid_rows * branch
            norm_two = low(normalize(middle))
            gate_rows = low_back(matmul(norm_two, gate_weight))
            upper_rows = low_back(matmul(norm_two, up_weight))
            hidden = low(jax.nn.silu(gate_rows) * upper_rows)
            feedforward = low_back(matmul(hidden, down_weight))
            return middle + valid_rows * feedforward
        layer_rows, pullback = jax.vjp(layer_forward, slot_tokens.astype(jnp.float32), weights[0], weights[1], weights[2], weights[3], weights[4], weights[5], weights[6])
        gradients = pullback(slot_cotangent.astype(jnp.float32) * valid_rows)
        new_sums = tuple((total + term for total, term in zip(gradient_sums, gradients[1:])))
        return (new_sums, (layer_rows.astype(jnp.bfloat16), gradients[0]))
    initial = tuple((jnp.zeros_like(weight) for weight in weights))
    gradient_sums, (layer_out, input_grad) = lax.scan(per_slot, initial, (tokens, lengths, cotangent))
    return (layer_out, input_grad, gradient_sums[0], gradient_sums[1], gradient_sums[2], gradient_sums[3], gradient_sums[4], gradient_sums[5], gradient_sums[6])
```

```python
import math

import jax
import jax.numpy as jnp
from jax import lax
from jax.sharding import PartitionSpec as P

HEAD_DIM = 128
ROWS = ("context", "tensor")


def rope_tables(positions, head_dim):
    half_dim = head_dim // 2
    inverse_freq = jnp.exp(
        -math.log(10000.0) * jnp.arange(half_dim, dtype=jnp.float32) * 2.0 / head_dim
    )
    angles = positions.astype(jnp.float32)[:, None] * inverse_freq[None, :]
    angles = jnp.concatenate([angles, angles], axis=-1)
    return (jnp.cos(angles)[:, None, :], jnp.sin(angles)[:, None, :])


def rotate(values, cosine, sine):
    half_dim = values.shape[-1] // 2
    turned = jnp.concatenate([-values[..., half_dim:], values[..., :half_dim]], axis=-1)
    return values * cosine + turned * sine


def unrotate(upstream, cosine, sine):
    half_dim = upstream.shape[-1] // 2
    scaled = upstream * sine
    turned = jnp.concatenate([scaled[..., half_dim:], -scaled[..., :half_dim]], axis=-1)
    return upstream * cosine + turned


def normalize(values):
    centered = values - jnp.mean(values, axis=-1, keepdims=True)
    inverse = lax.rsqrt(jnp.mean(centered * centered, axis=-1, keepdims=True) + 1e-05)
    return (centered * inverse, inverse)


def normalize_back(normed, inverse, upstream):
    mean_grad = jnp.mean(upstream, axis=-1, keepdims=True)
    mean_cross = jnp.mean(upstream * normed, axis=-1, keepdims=True)
    return inverse * (upstream - mean_grad - normed * mean_cross)


def dot(left, right, dims):
    return lax.dot_general(left, right, (dims, ((), ())), preferred_element_type=jnp.float32)


def gather_rows(values):
    return lax.all_gather(values, ROWS, axis=1, tiled=True)


def scatter_rows(values):
    return lax.psum_scatter(values, ROWS, scatter_dimension=1, tiled=True)


def column_weight(weight):
    moved = lax.all_to_all(weight, "context", split_axis=1, concat_axis=0, tiled=True)
    return lax.all_gather(moved, "dp", axis=0, tiled=True)


def row_weight(weight):
    moved = lax.all_to_all(weight, "context", split_axis=0, concat_axis=1, tiled=True)
    return lax.all_gather(moved, "dp", axis=1, tiled=True)


def column_gradient(partial):
    summed = lax.psum_scatter(partial, "dp", scatter_dimension=0, tiled=True)
    return lax.all_to_all(summed, "context", split_axis=0, concat_axis=1, tiled=True)


def row_gradient(partial):
    summed = lax.psum_scatter(partial, "dp", scatter_dimension=1, tiled=True)
    return lax.all_to_all(summed, "context", split_axis=1, concat_axis=0, tiled=True)


def per_device(tokens, lengths, w_query, w_key, w_value, w_out, w_gate, w_up, w_down, cotangent):
    low = jnp.bfloat16
    slots, chip_rows, width = tokens.shape
    contexts, cores = lax.axis_size("context"), lax.axis_size("tensor")
    rows = chip_rows // cores
    seq = chip_rows * contexts
    total = slots * seq
    heads = w_query.shape[1] // contexts // HEAD_DIM
    scale = 1.0 / math.sqrt(HEAD_DIM)
    core = lax.axis_index("tensor")
    own_start = lax.axis_index("context") * chip_rows + core * rows
    own_positions = own_start + jnp.arange(rows, dtype=jnp.int32)
    positions = jnp.arange(seq, dtype=jnp.int32)
    rope_cos, rope_sin = rope_tables(positions, HEAD_DIM)
    allowed = (positions[None, :] <= positions[:, None])[None] & (
        positions[None, None, :] < lengths[:, None, None]
    )
    allowed = allowed[:, None]
    valid_rows = (own_positions[None, :] < lengths[:, None]).astype(jnp.float32)[..., None]

    own_tokens = lax.dynamic_slice_in_dim(tokens, core * rows, rows, 1).astype(jnp.float32)
    own_cotangent = lax.dynamic_slice_in_dim(cotangent, core * rows, rows, 1).astype(jnp.float32)

    norm_one, inverse_one = normalize(own_tokens)
    norm_one_all = gather_rows(norm_one.astype(low)).reshape(total, width)
    query_w, key_w, value_w = (column_weight(w) for w in (w_query, w_key, w_value))
    out_w = row_weight(w_out)
    gate_w, up_w = (column_weight(w) for w in (w_gate, w_up))
    down_w = row_weight(w_down)
    out_grad = own_cotangent * valid_rows
    ffn_grad_all = gather_rows((valid_rows * out_grad).astype(low)).reshape(total, width)

    def split(values):
        return values.reshape(slots, seq, heads, HEAD_DIM)

    query = rotate(split(dot(norm_one_all, query_w, ((1,), (0,)))), rope_cos, rope_sin).astype(low)
    key = rotate(split(dot(norm_one_all, key_w, ((1,), (0,)))), rope_cos, rope_sin).astype(low)
    value = split(dot(norm_one_all, value_w, ((1,), (0,))).astype(low))

    def einsum(form, left, right):
        return jnp.einsum(form, left, right, preferred_element_type=jnp.float32)

    scores = einsum("sqhd,skhd->shqk", query, key) * scale
    masked = jnp.where(allowed, scores, -1e30)
    row_top = jnp.max(masked, axis=-1, keepdims=True)
    exponent = jnp.where(allowed, jnp.exp(masked - row_top), 0.0)
    probabilities = exponent / jnp.sum(exponent, axis=-1, keepdims=True)
    attended = einsum("shqk,skhd->sqhd", probabilities.astype(low), value)
    attended = attended.reshape(total, heads * HEAD_DIM).astype(low)

    branch = dot(attended, out_w, ((1,), (0,))).astype(low).reshape(slots, seq, width)
    branch = scatter_rows(branch).astype(jnp.float32)
    middle = own_tokens + valid_rows * branch
    norm_two, inverse_two = normalize(middle)
    norm_two_all = gather_rows(norm_two.astype(low)).reshape(total, width)

    gate = dot(norm_two_all, gate_w, ((1,), (0,)))
    upper = dot(norm_two_all, up_w, ((1,), (0,)))
    sigmoid = jax.nn.sigmoid(gate)
    silu = gate * sigmoid
    hidden = (silu * upper).astype(low)
    hidden_grad = dot(ffn_grad_all, down_w, ((1,), (1,)))
    gate_grad = (hidden_grad * upper * sigmoid * (1.0 + gate * (1.0 - sigmoid))).astype(low)
    upper_grad = (hidden_grad * silu).astype(low)
    norm_two_part = dot(gate_grad, gate_w, ((1,), (1,))) + dot(upper_grad, up_w, ((1,), (1,)))
    norm_two_grad = scatter_rows(norm_two_part.astype(low).reshape(slots, seq, width)).astype(
        jnp.float32
    )
    middle_grad = out_grad + normalize_back(norm_two, inverse_two, norm_two_grad)
    branch_grad_all = gather_rows((valid_rows * middle_grad).astype(low)).reshape(total, width)

    feedforward = dot(hidden, down_w, ((1,), (0,))).astype(low).reshape(slots, seq, width)
    feedforward = scatter_rows(feedforward).astype(jnp.float32)
    layer_out = (middle + valid_rows * feedforward).astype(low)
    layer_out = lax.all_gather(layer_out, "tensor", axis=1, tiled=True)

    grad_down = row_gradient(dot(hidden, ffn_grad_all, ((0,), (0,))).astype(low))
    grad_gate = column_gradient(dot(norm_two_all, gate_grad, ((0,), (0,))).astype(low))
    grad_up = column_gradient(dot(norm_two_all, upper_grad, ((0,), (0,))).astype(low))

    attended_grad = split(dot(branch_grad_all, out_w, ((1,), (1,))).astype(low))
    grad_out = row_gradient(dot(attended, branch_grad_all, ((0,), (0,))).astype(low))
    prob_grad = einsum("sqhd,skhd->shqk", attended_grad, value)
    row_delta = jnp.sum(probabilities * prob_grad, axis=-1, keepdims=True)
    score_grad = (probabilities * (prob_grad - row_delta)).astype(low)
    query_grad = einsum("shqk,skhd->sqhd", score_grad, key) * scale
    key_grad = einsum("shqk,sqhd->skhd", score_grad, query) * scale
    value_grad = einsum("shqk,sqhd->skhd", probabilities.astype(low), attended_grad)
    query_low = unrotate(query_grad, rope_cos, rope_sin).astype(low).reshape(total, -1)
    key_low = unrotate(key_grad, rope_cos, rope_sin).astype(low).reshape(total, -1)
    value_low = value_grad.astype(low).reshape(total, -1)
    norm_one_part = (
        dot(query_low, query_w, ((1,), (1,)))
        + dot(key_low, key_w, ((1,), (1,)))
        + dot(value_low, value_w, ((1,), (1,)))
    )
    norm_one_grad = scatter_rows(norm_one_part.astype(low).reshape(slots, seq, width)).astype(
        jnp.float32
    )
    input_grad = middle_grad + normalize_back(norm_one, inverse_one, norm_one_grad)
    input_grad = lax.all_gather(input_grad, "tensor", axis=1, tiled=True)
    grad_query = column_gradient(dot(norm_one_all, query_low, ((0,), (0,))).astype(low))
    grad_key = column_gradient(dot(norm_one_all, key_low, ((0,), (0,))).astype(low))
    grad_value = column_gradient(dot(norm_one_all, value_low, ((0,), (0,))).astype(low))
    grads = (grad_query, grad_key, grad_value, grad_out, grad_gate, grad_up, grad_down)
    return (layer_out, input_grad) + tuple(g.astype(jnp.float32) for g in grads)


def solution(mesh):
    tokens = P("dp", "context", None)
    column = P(("dp", "context"), "tensor")
    row = P("tensor", ("dp", "context"))
    weights = (column, column, column, row, column, column, row)
    return jax.shard_map(
        per_device,
        mesh=mesh,
        in_specs=(tokens, P("dp")) + weights + (tokens,),
        out_specs=(tokens, tokens) + weights,
        check_vma=False,
    )
```

```python
import math

import jax
import jax.numpy as jnp
from jax import lax
from jax.sharding import PartitionSpec as P

HEAD_DIM = 128
ROWS = ("context", "tensor")


def rope_tables(positions, head_dim):
    half_dim = head_dim // 2
    inverse_freq = jnp.exp(
        -math.log(10000.0) * jnp.arange(half_dim, dtype=jnp.float32) * 2.0 / head_dim
    )
    angles = positions.astype(jnp.float32)[:, None] * inverse_freq[None, :]
    angles = jnp.concatenate([angles, angles], axis=-1)
    return (jnp.cos(angles)[:, None, :], jnp.sin(angles)[:, None, :])


def rotate(values, cosine, sine):
    half_dim = values.shape[-1] // 2
    turned = jnp.concatenate([-values[..., half_dim:], values[..., :half_dim]], axis=-1)
    return values * cosine + turned * sine


def unrotate(upstream, cosine, sine):
    half_dim = upstream.shape[-1] // 2
    scaled = upstream * sine
    turned = jnp.concatenate([scaled[..., half_dim:], -scaled[..., :half_dim]], axis=-1)
    return upstream * cosine + turned


def normalize(values):
    centered = values - jnp.mean(values, axis=-1, keepdims=True)
    inverse = lax.rsqrt(jnp.mean(centered * centered, axis=-1, keepdims=True) + 1e-05)
    return (centered * inverse, inverse)


def normalize_back(normed, inverse, upstream):
    mean_grad = jnp.mean(upstream, axis=-1, keepdims=True)
    mean_cross = jnp.mean(upstream * normed, axis=-1, keepdims=True)
    return inverse * (upstream - mean_grad - normed * mean_cross)


def dot(left, right, dims):
    return lax.dot_general(left, right, (dims, ((), ())), preferred_element_type=jnp.float32)


def gather_rows(values):
    return lax.all_gather(values, ROWS, axis=0, tiled=True)


def scatter_rows(values):
    return lax.psum_scatter(values.astype(jnp.bfloat16), ROWS, scatter_dimension=0, tiled=True).astype(
        jnp.float32
    )


def put(buffer, piece, index):
    return lax.dynamic_update_slice_in_dim(buffer, piece[None], index, 0)


def take(buffer, index):
    return lax.dynamic_index_in_dim(buffer, index, 0, keepdims=False)


def spread_weight(weight):
    rows, contexts, columns = weight.shape
    groups = lax.axis_size("dp")
    here, group = lax.axis_index("context"), lax.axis_index("dp")
    pieces = jnp.moveaxis(weight, 1, 0)
    mine = jnp.zeros((contexts, rows, columns), weight.dtype)
    mine = put(mine, take(pieces, here), here)
    for step in range(1, contexts):
        route = [(i, (i + step) % contexts) for i in range(contexts)]
        piece = lax.ppermute(take(pieces, (here + step) % contexts), "context", route)
        mine = put(mine, piece, (here - step) % contexts)
    whole = jnp.zeros((groups,) + mine.shape, weight.dtype)
    whole = put(whole, mine, group)
    for step in range(1, groups):
        route = [(i, i ^ step) for i in range(groups)]
        whole = put(whole, lax.ppermute(mine, "dp", route), group ^ step)
    return whole.reshape(groups * contexts * rows, columns)


def collect_gradient(partial, contexts):
    groups = lax.axis_size("dp")
    here, group = lax.axis_index("context"), lax.axis_index("dp")
    columns = partial.shape[1]
    rows = partial.shape[0] // (groups * contexts)
    parts = partial.reshape(groups, contexts * rows, columns)
    total = take(parts, group).astype(jnp.float32)
    for step in range(1, groups):
        route = [(i, i ^ step) for i in range(groups)]
        total = total + lax.ppermute(take(parts, group ^ step), "dp", route).astype(jnp.float32)
    pieces = total.astype(jnp.bfloat16).reshape(contexts, rows, columns)
    mine = jnp.zeros_like(pieces)
    mine = put(mine, take(pieces, here), here)
    for step in range(1, contexts):
        route = [(i, (i + step) % contexts) for i in range(contexts)]
        piece = lax.ppermute(take(pieces, (here + step) % contexts), "context", route)
        mine = put(mine, piece, (here - step) % contexts)
    return jnp.moveaxis(mine, 0, 1)


def per_device(tokens, lengths, w_query, w_key, w_value, w_out, w_gate, w_up, w_down, cotangent):
    low = jnp.bfloat16
    slots, chip_rows, width = tokens.shape
    contexts, cores = lax.axis_size("context"), lax.axis_size("tensor")
    rows = chip_rows // cores
    seq = chip_rows * contexts
    head_cols = w_query.shape[1] // contexts
    units = w_gate.shape[1] // contexts
    heads = head_cols // HEAD_DIM
    scale = 1.0 / math.sqrt(HEAD_DIM)
    core = lax.axis_index("tensor")
    own_start = lax.axis_index("context") * chip_rows + core * rows
    own_positions = own_start + jnp.arange(rows, dtype=jnp.int32)
    positions = jnp.arange(seq, dtype=jnp.int32)
    rope_cos, rope_sin = rope_tables(positions, HEAD_DIM)
    causal = positions[None, :] <= positions[:, None]

    def by_context(weight):
        return weight.reshape(weight.shape[0], contexts, -1)

    attention_w = spread_weight(
        jnp.concatenate([by_context(w) for w in (w_query, w_key, w_value, w_out.T)], axis=2)
    )
    qkv_w, out_w = attention_w[:, : 3 * head_cols], attention_w[:, 3 * head_cols :]
    ffn_w = spread_weight(
        jnp.concatenate([by_context(w) for w in (w_gate, w_up, w_down.T)], axis=2)
    )
    gate_up_w, down_w = ffn_w[:, : 2 * units], ffn_w[:, 2 * units :]

    def einsum(form, left, right):
        return jnp.einsum(form, left, right, preferred_element_type=jnp.float32)

    def split(values):
        return values.reshape(seq, heads, HEAD_DIM)

    def slot_pass(slot):
        own_tokens = lax.dynamic_slice_in_dim(tokens[slot], core * rows, rows, 0).astype(jnp.float32)
        own_cotangent = lax.dynamic_slice_in_dim(cotangent[slot], core * rows, rows, 0).astype(
            jnp.float32
        )
        length = lengths[slot]
        valid_rows = (own_positions < length).astype(jnp.float32)[:, None]
        allowed = (causal & (positions < length)[None, :])[None]
        norm_one, inverse_one = normalize(own_tokens)
        norm_one_all = gather_rows(norm_one.astype(low))
        out_grad = own_cotangent * valid_rows
        ffn_grad_all = gather_rows((valid_rows * out_grad).astype(low))

        qkv = dot(norm_one_all, qkv_w, ((1,), (0,)))
        query, key, value = (qkv[:, i * head_cols : (i + 1) * head_cols] for i in range(3))
        query = rotate(split(query), rope_cos, rope_sin).astype(low)
        key = rotate(split(key), rope_cos, rope_sin).astype(low)
        value = split(value.astype(low))
        scores = einsum("qhd,khd->hqk", query, key) * scale
        masked = jnp.where(allowed, scores, -1e30)
        row_top = jnp.max(masked, axis=-1, keepdims=True)
        exponent = jnp.where(allowed, jnp.exp(masked - row_top), 0.0)
        probabilities = exponent / jnp.sum(exponent, axis=-1, keepdims=True)
        attended = einsum("hqk,khd->qhd", probabilities.astype(low), value)
        attended = attended.reshape(seq, heads * HEAD_DIM).astype(low)

        branch = scatter_rows(dot(attended, out_w, ((1,), (1,))))
        middle = own_tokens + valid_rows * branch
        norm_two, inverse_two = normalize(middle)
        norm_two_all = gather_rows(norm_two.astype(low))

        gate_up = dot(norm_two_all, gate_up_w, ((1,), (0,)))
        gate, upper = gate_up[:, :units], gate_up[:, units:]
        sigmoid = jax.nn.sigmoid(gate)
        silu = gate * sigmoid
        hidden = (silu * upper).astype(low)
        hidden_grad = dot(ffn_grad_all, down_w, ((1,), (0,)))
        gate_grad = (hidden_grad * upper * sigmoid * (1.0 + gate * (1.0 - sigmoid))).astype(low)
        upper_grad = (hidden_grad * silu).astype(low)
        gate_up_grad = jnp.concatenate([gate_grad, upper_grad], axis=1)
        norm_two_grad = scatter_rows(dot(gate_up_grad, gate_up_w, ((1,), (1,))))
        middle_grad = out_grad + normalize_back(norm_two, inverse_two, norm_two_grad)
        branch_grad_all = gather_rows((valid_rows * middle_grad).astype(low))

        feedforward = scatter_rows(dot(hidden, down_w, ((1,), (1,))))
        layer_out = (middle + valid_rows * feedforward).astype(low)
        ffn_grads = (dot(norm_two_all, gate_up_grad, ((0,), (0,))), dot(ffn_grad_all, hidden, ((0,), (0,))))

        attended_grad = split(dot(branch_grad_all, out_w, ((1,), (0,))).astype(low))
        grad_out = dot(branch_grad_all, attended, ((0,), (0,)))
        prob_grad = einsum("qhd,khd->hqk", attended_grad, value)
        row_delta = jnp.sum(probabilities * prob_grad, axis=-1, keepdims=True)
        score_grad = (probabilities * (prob_grad - row_delta)).astype(low)
        query_grad = einsum("hqk,khd->qhd", score_grad, key) * scale
        key_grad = einsum("hqk,qhd->khd", score_grad, query) * scale
        value_grad = einsum("hqk,qhd->khd", probabilities.astype(low), attended_grad)
        qkv_grad = jnp.concatenate(
            [
                unrotate(query_grad, rope_cos, rope_sin).astype(low).reshape(seq, -1),
                unrotate(key_grad, rope_cos, rope_sin).astype(low).reshape(seq, -1),
                value_grad.astype(low).reshape(seq, -1),
            ],
            axis=1,
        )
        norm_one_grad = scatter_rows(dot(qkv_grad, qkv_w, ((1,), (1,))))
        input_grad = middle_grad + normalize_back(norm_one, inverse_one, norm_one_grad)
        attention_grads = (dot(norm_one_all, qkv_grad, ((0,), (0,))), grad_out)
        return layer_out, input_grad, attention_grads, ffn_grads

    results = [slot_pass(slot) for slot in range(slots)]
    layer_out = lax.all_gather(jnp.stack([r[0] for r in results]), "tensor", axis=1, tiled=True)
    input_grad = lax.all_gather(jnp.stack([r[1] for r in results]), "tensor", axis=1, tiled=True)

    def summed(group, item):
        total = results[0][group][item]
        for other in results[1:]:
            total = total + other[group][item]
        return total.astype(low)

    attention = collect_gradient(jnp.concatenate([summed(2, 0), summed(2, 1)], axis=1), contexts)
    ffn = collect_gradient(jnp.concatenate([summed(3, 0), summed(3, 1)], axis=1), contexts)
    attention, ffn = attention.astype(jnp.float32), ffn.astype(jnp.float32)

    def piece(array, start, size):
        return array[:, :, start : start + size].reshape(array.shape[0], -1)

    grads = tuple(piece(attention, i * head_cols, head_cols) for i in range(3)) + (
        piece(attention, 3 * head_cols, head_cols).T,
        piece(ffn, 0, units),
        piece(ffn, units, units),
        piece(ffn, 2 * units, units).T,
    )
    return (layer_out, input_grad) + grads


def solution(mesh):
    tokens = P("dp", "context", None)
    column = P(("dp", "context"), "tensor")
    row = P("tensor", ("dp", "context"))
    weights = (column, column, column, row, column, column, row)
    return jax.shard_map(
        per_device,
        mesh=mesh,
        in_specs=(tokens, P("dp")) + weights + (tokens,),
        out_specs=(tokens, tokens) + weights,
        check_vma=False,
    )
```

```python
import math

import jax
import jax.numpy as jnp
from jax import lax
from jax.sharding import PartitionSpec as P

HEAD_DIM = 128
SEQUENCE_ROWS = ("context", "tensor")
PLANE_ROWS = ("dp", "tensor")


def rope_tables(positions, head_dim):
    half_dim = head_dim // 2
    inverse_freq = jnp.exp(
        -math.log(10000.0) * jnp.arange(half_dim, dtype=jnp.float32) * 2.0 / head_dim
    )
    angles = positions.astype(jnp.float32)[:, None] * inverse_freq[None, :]
    angles = jnp.concatenate([angles, angles], axis=-1)
    return (jnp.cos(angles)[:, None, :], jnp.sin(angles)[:, None, :])


def rotate(values, cosine, sine):
    half_dim = values.shape[-1] // 2
    turned = jnp.concatenate([-values[..., half_dim:], values[..., :half_dim]], axis=-1)
    return values * cosine + turned * sine


def unrotate(upstream, cosine, sine):
    half_dim = upstream.shape[-1] // 2
    scaled = upstream * sine
    turned = jnp.concatenate([scaled[..., half_dim:], -scaled[..., :half_dim]], axis=-1)
    return upstream * cosine + turned


def normalize(values):
    centered = values - jnp.mean(values, axis=-1, keepdims=True)
    inverse = lax.rsqrt(jnp.mean(centered * centered, axis=-1, keepdims=True) + 1e-05)
    return (centered * inverse, inverse)


def normalize_back(normed, inverse, upstream):
    mean_grad = jnp.mean(upstream, axis=-1, keepdims=True)
    mean_cross = jnp.mean(upstream * normed, axis=-1, keepdims=True)
    return inverse * (upstream - mean_grad - normed * mean_cross)


def dot(left, right, dims):
    return lax.dot_general(left, right, (dims, ((), ())), preferred_element_type=jnp.float32)


def gather_rows(values, axes):
    return lax.all_gather(values, axes, axis=0, tiled=True)


def scatter_rows(values, axes):
    return lax.psum_scatter(values.astype(jnp.bfloat16), axes, scatter_dimension=0, tiled=True).astype(
        jnp.float32
    )


def join_cores(values):
    cores = lax.axis_size("tensor")
    core, rows = lax.axis_index("tensor"), values.shape[1]
    whole = jnp.concatenate([values] * cores, axis=1)
    for step in range(1, cores):
        route = [(i, (i + step) % cores) for i in range(cores)]
        other = lax.ppermute(values, "tensor", route)
        whole = lax.dynamic_update_slice_in_dim(whole, other, ((core - step) % cores) * rows, 1)
    return whole


def put(buffer, piece, index):
    return lax.dynamic_update_slice_in_dim(buffer, piece[None], index, 0)


def take(buffer, index):
    return lax.dynamic_index_in_dim(buffer, index, 0, keepdims=False)


def spread_weight(weight):
    rows, contexts, columns = weight.shape
    groups = lax.axis_size("dp")
    here, group = lax.axis_index("context"), lax.axis_index("dp")
    pieces = jnp.moveaxis(weight, 1, 0)
    mine = jnp.zeros((contexts, rows, columns), weight.dtype)
    mine = put(mine, take(pieces, here), here)
    for step in range(1, contexts):
        route = [(i, (i + step) % contexts) for i in range(contexts)]
        piece = lax.ppermute(take(pieces, (here + step) % contexts), "context", route)
        mine = put(mine, piece, (here - step) % contexts)
    whole = jnp.zeros((groups,) + mine.shape, weight.dtype)
    whole = put(whole, mine, group)
    for step in range(1, groups):
        route = [(i, i ^ step) for i in range(groups)]
        whole = put(whole, lax.ppermute(mine, "dp", route), group ^ step)
    return whole.reshape(groups * contexts * rows, columns)


def collect_pieces(partial, contexts):
    groups = lax.axis_size("dp")
    group = lax.axis_index("dp")
    columns = partial.shape[1]
    rows = partial.shape[0] // (groups * contexts)
    parts = partial.reshape(groups, contexts * rows, columns)
    total = take(parts, group).astype(jnp.float32)
    for step in range(1, groups):
        route = [(i, i ^ step) for i in range(groups)]
        total = total + lax.ppermute(take(parts, group ^ step), "dp", route).astype(jnp.float32)
    return swap(total.astype(jnp.bfloat16).reshape(contexts, rows, columns), "context")


def swap(pieces, axis):
    members, here = lax.axis_size(axis), lax.axis_index(axis)
    arrived = [take(pieces, here)]
    for step in range(1, members):
        route = [(i, i ^ step) for i in range(members)]
        arrived.append(lax.ppermute(take(pieces, here ^ step), axis, route))
    return arrived


def exchange(pieces, axis):
    here = lax.axis_index(axis)
    mine = jnp.zeros_like(pieces)
    for step, piece in enumerate(swap(pieces, axis)):
        mine = put(mine, piece, here ^ step)
    return mine


def relay_hops(block):
    n = lax.axis_size("context")
    up, down = [], []
    moving_up = moving_down = block
    for step in range(1, n):
        moving_up = lax.ppermute(moving_up, "context", [(i, i + 1) for i in range(step - 1, n - 1)])
        moving_down = lax.ppermute(moving_down, "context", [(i, i - 1) for i in range(1, n - step + 1)])
        up.append(moving_up)
        down.append(moving_down)
    return up, down


def hold(value, hops, index):
    up, down = hops
    if index < len(up):
        value, up[index], down[index] = lax.optimization_barrier((value, up[index], down[index]))
    return value


def assemble(block, hops):
    n, here = lax.axis_size("context"), lax.axis_index("context")
    up, down = hops
    groups, rows, columns = block.shape
    whole = jnp.zeros((groups, n, rows, columns), block.dtype)
    whole = lax.dynamic_update_slice_in_dim(whole, block[:, None], here, 1)
    for step in range(1, n):
        piece = jnp.where(here >= step, up[step - 1], down[n - step - 1])
        whole = lax.dynamic_update_slice_in_dim(whole, piece[:, None], (here - step) % n, 1)
    return whole.reshape(-1, columns)


def scatter_plane(values):
    low = jnp.bfloat16
    cores, groups = lax.axis_size("tensor"), lax.axis_size("dp")
    core, group = lax.axis_index("tensor"), lax.axis_index("dp")
    width = values.shape[1]
    parts = values.astype(low).reshape(groups, cores, -1, width)

    def of_core(index):
        return lax.dynamic_index_in_dim(parts, index % cores, 1, keepdims=False)

    total = of_core(core).astype(jnp.float32)
    for step in range(1, cores):
        route = [(i, (i + step) % cores) for i in range(cores)]
        total = total + lax.ppermute(of_core(core + step), "tensor", route).astype(jnp.float32)
    total = total.astype(low)
    bits = list(range(groups.bit_length() - 1))
    results = []
    for part, order in enumerate((bits, bits[::-1])):
        half = width // 2
        block = total[:, :, part * half : (part + 1) * half]
        rows = block.shape[1]
        block = block.reshape((2,) * len(bits) + (rows, half))
        left = bits[::-1]
        for bit in order:
            axis, mine = left.index(bit), (group >> bit) & 1
            keep = lax.dynamic_index_in_dim(block, mine, axis, keepdims=False)
            send = lax.dynamic_index_in_dim(block, 1 - mine, axis, keepdims=False)
            route = [(i, i ^ (1 << bit)) for i in range(groups)]
            other = lax.ppermute(send, "dp", route)
            block = keep.astype(jnp.float32) + other.astype(jnp.float32)
            left.remove(bit)
            if left:
                block = block.astype(low)
        results.append(block)
    return jnp.concatenate(results, axis=1)


class Reduction:
    def __init__(self, partial, groups, contexts):
        self.parts = partial.reshape(groups, contexts, -1, partial.shape[1])
        self.n, self.here = contexts, lax.axis_index("context")
        self.above = self.below = None
        self.step = 0

    def term(self, index):
        picked = lax.dynamic_index_in_dim(self.parts, index % self.n, 1, keepdims=False)
        return picked.astype(jnp.float32)

    def hop(self):
        if self.step == self.n - 1:
            return
        self.step += 1
        step, n = self.step, self.n
        above, below = self.term(self.here - step), self.term(self.here + step)
        if self.above is not None:
            above, below = above + self.above.astype(jnp.float32), below + self.below.astype(jnp.float32)
        self.above = lax.ppermute(
            above.astype(jnp.bfloat16), "context", [(i, i + 1) for i in range(min(step, n - 1))]
        )
        self.below = lax.ppermute(
            below.astype(jnp.bfloat16), "context", [(i, i - 1) for i in range(max(1, n - step), n)]
        )

    def hold(self, value):
        value, self.above, self.below = lax.optimization_barrier((value, self.above, self.below))
        return value

    def finish(self):
        while self.step < self.n - 1:
            self.hop()
        total = self.term(self.here) + self.above.astype(jnp.float32) + self.below.astype(jnp.float32)
        return swap(total.astype(jnp.bfloat16), "dp")


def per_device(tokens, lengths, w_query, w_key, w_value, w_out, w_gate, w_up, w_down, cotangent):
    low = jnp.bfloat16
    slots, chip_rows, width = tokens.shape
    contexts, cores = lax.axis_size("context"), lax.axis_size("tensor")
    rows = chip_rows // cores
    seq = chip_rows * contexts
    head_cols = w_query.shape[1] // contexts
    groups = lax.axis_size("dp")
    units = w_gate.shape[1] // groups
    heads = head_cols // HEAD_DIM
    scale = 1.0 / math.sqrt(HEAD_DIM)
    core = lax.axis_index("tensor")
    own_start = lax.axis_index("context") * chip_rows + core * rows
    own_positions = own_start + jnp.arange(rows, dtype=jnp.int32)
    positions = jnp.arange(seq, dtype=jnp.int32)
    rope_cos, rope_sin = rope_tables(positions, HEAD_DIM)
    causal = positions[None, :] <= positions[:, None]

    def by_context(weight):
        return weight.reshape(weight.shape[0], contexts, -1)

    attention_w = spread_weight(
        jnp.concatenate([by_context(w) for w in (w_query, w_key, w_value, w_out.T)], axis=2)
    )
    qkv_w, out_w = attention_w[:, : 3 * head_cols], attention_w[:, 3 * head_cols :]

    def by_group(weight):
        return jnp.moveaxis(weight.reshape(weight.shape[0], groups, -1), 1, 0)

    gate_up_block = exchange(jnp.concatenate([by_group(w_gate), by_group(w_up)], axis=2), "dp")
    down_block = exchange(by_group(w_down.T), "dp")

    def einsum(form, left, right):
        return jnp.einsum(form, left, right, preferred_element_type=jnp.float32)

    def split(values):
        return values.reshape(seq, heads, HEAD_DIM)

    def own(array, slot):
        return lax.dynamic_slice_in_dim(array[slot], core * rows, rows, 0).astype(jnp.float32)

    each = range(slots)
    own_tokens = [own(tokens, slot) for slot in each]
    valid_rows = [(own_positions < lengths[slot]).astype(jnp.float32)[:, None] for slot in each]
    allowed = [(causal & (positions < lengths[slot])[None, :])[None] for slot in each]
    out_grad = [own(cotangent, slot) * valid_rows[slot] for slot in each]
    ffn_grad = [(valid_rows[slot] * out_grad[slot]).astype(low) for slot in each]
    norm_one, inverse_one = zip(*[normalize(own_tokens[slot]) for slot in each])
    norm_one_all = [gather_rows(norm_one[slot].astype(low), SEQUENCE_ROWS) for slot in each]

    norm_one_all[0], gate_up_block, down_block = lax.optimization_barrier(
        (norm_one_all[0], gate_up_block, down_block)
    )
    gate_up_hops, down_hops = relay_hops(gate_up_block), relay_hops(down_block)
    last = slots - 1
    norm_one_all[last], *ffn_grad = lax.optimization_barrier((norm_one_all[last], *ffn_grad))
    ffn_grad_all = [gather_rows(ffn_grad[slot], PLANE_ROWS) for slot in each]
    norm_one_all[last] = hold(norm_one_all[last], gate_up_hops, 0)

    def attend(slot):
        qkv = dot(norm_one_all[slot], qkv_w, ((1,), (0,)))
        query, key, value = (qkv[:, i * head_cols : (i + 1) * head_cols] for i in range(3))
        query = rotate(split(query), rope_cos, rope_sin).astype(low)
        key = rotate(split(key), rope_cos, rope_sin).astype(low)
        value = split(value.astype(low))
        scores = einsum("qhd,khd->hqk", query, key) * scale
        masked = jnp.where(allowed[slot], scores, -1e30)
        row_top = jnp.max(masked, axis=-1, keepdims=True)
        exponent = jnp.where(allowed[slot], jnp.exp(masked - row_top), 0.0)
        probabilities = exponent / jnp.sum(exponent, axis=-1, keepdims=True)
        attended = einsum("hqk,khd->qhd", probabilities.astype(low), value)
        attended = attended.reshape(seq, heads * HEAD_DIM).astype(low)
        return query, key, value, probabilities, attended

    saved, branch = [], []
    for slot in each:
        kept = attend(slot)
        attended = kept[4]
        if slot == 0:
            attended, *ffn_grad_all = lax.optimization_barrier((attended, *ffn_grad_all))
        if slot == last:
            attended = hold(attended, gate_up_hops, 1)
        saved.append(kept[:4] + (attended,))
        branch.append(scatter_rows(dot(attended, out_w, ((1,), (1,))), SEQUENCE_ROWS))
    middle, norm_two, inverse_two, norm_two_all = [], [], [], []
    for slot in each:
        summed_branch = branch[slot]
        if slot == 0:
            summed_branch = hold(summed_branch, gate_up_hops, 2)
        if slot == last:
            summed_branch = hold(summed_branch, down_hops, 0)
        middle.append(own_tokens[slot] + valid_rows[slot] * summed_branch)
        normed, inverse = normalize(middle[slot])
        norm_two.append(normed)
        inverse_two.append(inverse)
        norm_two_all.append(gather_rows(normed.astype(low), PLANE_ROWS))
    for slot in each:
        norm_two_all[slot] = hold(norm_two_all[slot], down_hops, 1 + slot)
    gate_up_w, down_w = assemble(gate_up_block, gate_up_hops), assemble(down_block, down_hops)

    hidden, gate_up_grad, norm_two_grad = [], [], []
    for slot in each:
        gate_up = dot(norm_two_all[slot], gate_up_w, ((1,), (0,)))
        gate, upper = gate_up[:, :units], gate_up[:, units:]
        sigmoid = jax.nn.sigmoid(gate)
        silu = gate * sigmoid
        hidden.append((silu * upper).astype(low))
        hidden_grad = dot(ffn_grad_all[slot], down_w, ((1,), (0,)))
        gate_grad = (hidden_grad * upper * sigmoid * (1.0 + gate * (1.0 - sigmoid))).astype(low)
        upper_grad = (hidden_grad * silu).astype(low)
        gate_up_grad.append(jnp.concatenate([gate_grad, upper_grad], axis=1))
        norm_two_grad.append(scatter_plane(dot(gate_up_grad[slot], gate_up_w, ((1,), (1,)))))

    def over_slots(terms):
        total = terms[0]
        for other in terms[1:]:
            total = total + other
        return total.astype(low)

    down_sum = over_slots([dot(ffn_grad_all[slot], hidden[slot], ((0,), (0,))) for slot in each])
    down_sum = Reduction(down_sum, groups, contexts)
    gate_up_sum = over_slots([dot(norm_two_all[slot], gate_up_grad[slot], ((0,), (0,))) for slot in each])
    gate_up_sum = Reduction(gate_up_sum, groups, contexts)

    middle_grad, branch_grad_all = [], []
    for slot in each:
        upstream = norm_two_grad[slot]
        if slot == last:
            down_sum.hop()
            upstream = down_sum.hold(upstream)
        middle_grad.append(
            out_grad[slot] + normalize_back(norm_two[slot], inverse_two[slot], upstream)
        )
        branch_grad_all.append(
            gather_rows((valid_rows[slot] * middle_grad[slot]).astype(low), SEQUENCE_ROWS)
        )
    down_sum.hop()
    branch_grad_all[0] = down_sum.hold(branch_grad_all[0])
    down_sum.hop()
    gate_up_sum.hop()
    branch_grad_all[last] = down_sum.hold(gate_up_sum.hold(branch_grad_all[last]))
    branch_grad_all[last], *hidden_late = lax.optimization_barrier((branch_grad_all[last], *hidden))

    qkv_grad, norm_one_grad = [], []
    for slot in each:
        query, key, value, probabilities, attended = saved[slot]
        attended_grad = split(dot(branch_grad_all[slot], out_w, ((1,), (0,))).astype(low))
        prob_grad = einsum("qhd,khd->hqk", attended_grad, value)
        row_delta = jnp.sum(probabilities * prob_grad, axis=-1, keepdims=True)
        score_grad = (probabilities * (prob_grad - row_delta)).astype(low)
        query_grad = einsum("hqk,khd->qhd", score_grad, key) * scale
        key_grad = einsum("hqk,qhd->khd", score_grad, query) * scale
        value_grad = einsum("hqk,qhd->khd", probabilities.astype(low), attended_grad)
        qkv_grad.append(
            jnp.concatenate(
                [
                    unrotate(query_grad, rope_cos, rope_sin).astype(low).reshape(seq, -1),
                    unrotate(key_grad, rope_cos, rope_sin).astype(low).reshape(seq, -1),
                    value_grad.astype(low).reshape(seq, -1),
                ],
                axis=1,
            )
        )
        if slot == last:
            gate_up_sum.hop()
            qkv_grad[slot] = gate_up_sum.hold(qkv_grad[slot])
        norm_one_grad.append(
            scatter_rows(dot(qkv_grad[slot], qkv_w, ((1,), (1,))), SEQUENCE_ROWS)
        )
    out_sum = over_slots([dot(branch_grad_all[slot], saved[slot][4], ((0,), (0,))) for slot in each])
    qkv_sum = over_slots([dot(norm_one_all[slot], qkv_grad[slot], ((0,), (0,))) for slot in each])

    layer_out, input_grad = [], []
    for slot in each:
        feedforward = scatter_plane(dot(hidden_late[slot], down_w, ((1,), (1,))))
        layer_out.append((middle[slot] + valid_rows[slot] * feedforward).astype(low))
    gate_up_sum.hop()
    norm_one_grad[0] = gate_up_sum.hold(norm_one_grad[0])
    down_pieces = down_sum.finish()
    norm_one_grad[last], *rest = lax.optimization_barrier((norm_one_grad[last], *layer_out, *down_pieces))
    layer_out, down_pieces = rest[:slots], rest[slots:]
    for slot in each:
        upstream = norm_one_grad[slot]
        input_grad.append(
            middle_grad[slot] + normalize_back(norm_one[slot], inverse_one[slot], upstream)
        )
    layer_out, input_grad = join_cores(jnp.stack(layer_out)), join_cores(jnp.stack(input_grad))

    gate_up_pieces = gate_up_sum.finish()
    out_pieces = collect_pieces(out_sum, contexts)
    qkv_pieces = collect_pieces(qkv_sum, contexts)

    def column_output(pieces, axis, start, size):
        members, here = lax.axis_size(axis), lax.axis_index(axis)
        whole = jnp.zeros((pieces[0].shape[0], members * size), jnp.float32)
        for step, piece in enumerate(pieces):
            block = piece[:, start : start + size].astype(jnp.float32)
            whole = lax.dynamic_update_slice_in_dim(whole, block, (here ^ step) * size, 1)
        return whole

    def row_output(pieces, axis, size):
        members, here = lax.axis_size(axis), lax.axis_index(axis)
        whole = jnp.zeros((members * size, pieces[0].shape[0]), jnp.float32)
        for step, piece in enumerate(pieces):
            block = piece.astype(jnp.float32).T
            whole = lax.dynamic_update_slice_in_dim(whole, block, (here ^ step) * size, 0)
        return whole

    grads = tuple(column_output(qkv_pieces, "context", i * head_cols, head_cols) for i in range(3)) + (
        row_output(out_pieces, "context", head_cols),
        column_output(gate_up_pieces, "dp", 0, units),
        column_output(gate_up_pieces, "dp", units, units),
        row_output(down_pieces, "dp", units),
    )
    return (layer_out, input_grad) + grads


def solution(mesh):
    tokens = P("dp", "context", None)
    column = P(("dp", "context"), "tensor")
    row = P("tensor", ("dp", "context"))
    weights = (column, column, column, row, column, column, row)
    return jax.shard_map(
        per_device,
        mesh=mesh,
        in_specs=(tokens, P("dp")) + weights + (tokens,),
        out_specs=(tokens, tokens) + weights,
        check_vma=False,
    )
```

```python
import math

import jax
import jax.numpy as jnp
from jax import lax
from jax.sharding import PartitionSpec as P

HEAD_DIM = 128
SEQUENCE_ROWS = ("context", "tensor")
PLANE_ROWS = ("dp", "tensor")


def rope_tables(positions, head_dim):
    half_dim = head_dim // 2
    inverse_freq = jnp.exp(
        -math.log(10000.0) * jnp.arange(half_dim, dtype=jnp.float32) * 2.0 / head_dim
    )
    angles = positions.astype(jnp.float32)[:, None] * inverse_freq[None, :]
    angles = jnp.concatenate([angles, angles], axis=-1)
    return (jnp.cos(angles)[:, None, :], jnp.sin(angles)[:, None, :])


def rotate(values, cosine, sine):
    half_dim = values.shape[-1] // 2
    turned = jnp.concatenate([-values[..., half_dim:], values[..., :half_dim]], axis=-1)
    return values * cosine + turned * sine


def unrotate(upstream, cosine, sine):
    half_dim = upstream.shape[-1] // 2
    scaled = upstream * sine
    turned = jnp.concatenate([scaled[..., half_dim:], -scaled[..., :half_dim]], axis=-1)
    return upstream * cosine + turned


def normalize(values):
    centered = values - jnp.mean(values, axis=-1, keepdims=True)
    inverse = lax.rsqrt(jnp.mean(centered * centered, axis=-1, keepdims=True) + 1e-05)
    return (centered * inverse, inverse)


def normalize_back(normed, inverse, upstream):
    mean_grad = jnp.mean(upstream, axis=-1, keepdims=True)
    mean_cross = jnp.mean(upstream * normed, axis=-1, keepdims=True)
    return inverse * (upstream - mean_grad - normed * mean_cross)


def dot(left, right, dims):
    return lax.dot_general(left, right, (dims, ((), ())), preferred_element_type=jnp.float32)


def gather_rows(values, axes):
    return lax.all_gather(values, axes, axis=0, tiled=True)


def scatter_rows(values, axes):
    return lax.psum_scatter(values.astype(jnp.bfloat16), axes, scatter_dimension=0, tiled=True).astype(
        jnp.float32
    )


def join_cores(values):
    cores = lax.axis_size("tensor")
    core, rows = lax.axis_index("tensor"), values.shape[1]
    whole = jnp.concatenate([values] * cores, axis=1)
    for step in range(1, cores):
        route = [(i, (i + step) % cores) for i in range(cores)]
        other = lax.ppermute(values, "tensor", route)
        whole = lax.dynamic_update_slice_in_dim(whole, other, ((core - step) % cores) * rows, 1)
    return whole


def put(buffer, piece, index):
    return lax.dynamic_update_slice_in_dim(buffer, piece[None], index, 0)


def take(buffer, index):
    return lax.dynamic_index_in_dim(buffer, index, 0, keepdims=False)


def trade(weight, axis):
    return exchange(jnp.moveaxis(weight, 1, 0), axis)


def gather_groups(mine):
    group, groups = lax.axis_index("dp"), lax.axis_size("dp")
    whole = jnp.zeros((groups,) + mine.shape, mine.dtype)
    whole = put(whole, mine, group)
    for step in range(1, groups):
        route = [(i, i ^ step) for i in range(groups)]
        whole = put(whole, lax.ppermute(mine, "dp", route), group ^ step)
    return whole.reshape(-1, mine.shape[-1])


def reduce_groups(partials):
    group, groups = lax.axis_index("dp"), lax.axis_size("dp")
    parts = [partial.reshape(groups, -1, partial.shape[1]) for partial in partials]

    def term(index):
        return jnp.concatenate([take(part, index) for part in parts], axis=1)

    total = term(group).astype(jnp.float32)
    for step in range(1, groups):
        route = [(i, i ^ step) for i in range(groups)]
        total = total + lax.ppermute(term(group ^ step), "dp", route).astype(jnp.float32)
    return total.astype(jnp.bfloat16)


def swap(pieces, axis):
    members, here = lax.axis_size(axis), lax.axis_index(axis)
    arrived = [take(pieces, here)]
    for step in range(1, members):
        route = [(i, i ^ step) for i in range(members)]
        arrived.append(lax.ppermute(take(pieces, here ^ step), axis, route))
    return arrived


def exchange(pieces, axis):
    here = lax.axis_index(axis)
    mine = jnp.zeros_like(pieces)
    for step, piece in enumerate(swap(pieces, axis)):
        mine = put(mine, piece, here ^ step)
    return mine


def relay_hops(block):
    n = lax.axis_size("context")
    up, down = [], []
    moving_up = moving_down = block
    for step in range(1, n):
        moving_up = lax.ppermute(moving_up, "context", [(i, i + 1) for i in range(step - 1, n - 1)])
        moving_down = lax.ppermute(moving_down, "context", [(i, i - 1) for i in range(1, n - step + 1)])
        up.append(moving_up)
        down.append(moving_down)
    return up, down


def hold(value, hops, index):
    up, down = hops
    if index < len(up):
        value, up[index], down[index] = lax.optimization_barrier((value, up[index], down[index]))
    return value


def assemble(block, hops):
    n, here = lax.axis_size("context"), lax.axis_index("context")
    up, down = hops
    groups, rows, columns = block.shape
    whole = jnp.zeros((groups, n, rows, columns), block.dtype)
    whole = lax.dynamic_update_slice_in_dim(whole, block[:, None], here, 1)
    for step in range(1, n):
        piece = jnp.where(here >= step, up[step - 1], down[n - step - 1])
        whole = lax.dynamic_update_slice_in_dim(whole, piece[:, None], (here - step) % n, 1)
    return whole.reshape(-1, columns)


def scatter_plane(values):
    low = jnp.bfloat16
    cores, groups = lax.axis_size("tensor"), lax.axis_size("dp")
    core, group = lax.axis_index("tensor"), lax.axis_index("dp")
    width = values.shape[1]
    parts = values.astype(low).reshape(groups, cores, -1, width)

    def of_core(index):
        return lax.dynamic_index_in_dim(parts, index % cores, 1, keepdims=False)

    total = of_core(core).astype(jnp.float32)
    for step in range(1, cores):
        route = [(i, (i + step) % cores) for i in range(cores)]
        total = total + lax.ppermute(of_core(core + step), "tensor", route).astype(jnp.float32)
    total = total.astype(low)
    bits = list(range(groups.bit_length() - 1))
    results = []
    for part, order in enumerate((bits, bits[::-1])):
        half = width // 2
        block = total[:, :, part * half : (part + 1) * half]
        rows = block.shape[1]
        block = block.reshape((2,) * len(bits) + (rows, half))
        left = bits[::-1]
        for bit in order:
            axis, mine = left.index(bit), (group >> bit) & 1
            keep = lax.dynamic_index_in_dim(block, mine, axis, keepdims=False)
            send = lax.dynamic_index_in_dim(block, 1 - mine, axis, keepdims=False)
            route = [(i, i ^ (1 << bit)) for i in range(groups)]
            other = lax.ppermute(send, "dp", route)
            block = keep.astype(jnp.float32) + other.astype(jnp.float32)
            left.remove(bit)
            if left:
                block = block.astype(low)
        results.append(block)
    return jnp.concatenate(results, axis=1)


class Reduction:
    def __init__(self, partials, groups, contexts):
        self.parts = [partial.reshape(groups, contexts, -1, partial.shape[1]) for partial in partials]
        self.n, self.here = contexts, lax.axis_index("context")
        self.above = self.below = None
        self.step = 0

    def term(self, index):
        picked = [lax.dynamic_index_in_dim(part, index % self.n, 1, keepdims=False) for part in self.parts]
        return jnp.concatenate(picked, axis=-1).astype(jnp.float32)

    def hop(self):
        if self.step == self.n - 1:
            return
        self.step += 1
        step, n = self.step, self.n
        above, below = self.term(self.here - step), self.term(self.here + step)
        if self.above is not None:
            above, below = above + self.above.astype(jnp.float32), below + self.below.astype(jnp.float32)
        self.above = lax.ppermute(
            above.astype(jnp.bfloat16), "context", [(i, i + 1) for i in range(min(step, n - 1))]
        )
        self.below = lax.ppermute(
            below.astype(jnp.bfloat16), "context", [(i, i - 1) for i in range(max(1, n - step), n)]
        )

    def hold(self, value):
        value, self.above, self.below = lax.optimization_barrier((value, self.above, self.below))
        return value

    def finish(self):
        while self.step < self.n - 1:
            self.hop()
        total = self.term(self.here) + self.above.astype(jnp.float32) + self.below.astype(jnp.float32)
        return swap(total.astype(jnp.bfloat16), "dp")


def per_device(tokens, lengths, w_query, w_key, w_value, w_out, w_gate, w_up, w_down, cotangent):
    low = jnp.bfloat16
    slots, chip_rows, width = tokens.shape
    contexts, cores = lax.axis_size("context"), lax.axis_size("tensor")
    rows = chip_rows // cores
    seq = chip_rows * contexts
    head_cols = w_query.shape[1] // contexts
    groups = lax.axis_size("dp")
    units = w_gate.shape[1] // groups
    heads = head_cols // HEAD_DIM
    scale = 1.0 / math.sqrt(HEAD_DIM)
    core = lax.axis_index("tensor")
    own_start = lax.axis_index("context") * chip_rows + core * rows
    own_positions = own_start + jnp.arange(rows, dtype=jnp.int32)
    positions = jnp.arange(seq, dtype=jnp.int32)
    rope_cos, rope_sin = rope_tables(positions, HEAD_DIM)
    causal = positions[None, :] <= positions[:, None]

    def by_context(weight):
        return weight.reshape(weight.shape[0], contexts, -1)

    attention_part = trade(
        jnp.concatenate([by_context(w) for w in (w_query, w_key, w_value, w_out.T)], axis=2), "context"
    )

    def by_group(weight):
        return jnp.moveaxis(weight.reshape(weight.shape[0], groups, -1), 1, 0)

    ffn_block = exchange(
        jnp.concatenate([by_group(w) for w in (w_gate, w_up, w_down.T)], axis=2), "dp"
    )

    def einsum(form, left, right):
        return jnp.einsum(form, left, right, preferred_element_type=jnp.float32)

    def split(values):
        return values.reshape(seq, heads, HEAD_DIM)

    def own(array, slot):
        return lax.dynamic_slice_in_dim(array[slot], core * rows, rows, 0).astype(jnp.float32)

    each = range(slots)
    own_tokens = [own(tokens, slot) for slot in each]
    valid_rows = [(own_positions < lengths[slot]).astype(jnp.float32)[:, None] for slot in each]
    allowed = [(causal & (positions < lengths[slot])[None, :])[None] for slot in each]
    out_grad = [own(cotangent, slot) * valid_rows[slot] for slot in each]
    ffn_grad = [(valid_rows[slot] * out_grad[slot]).astype(low) for slot in each]
    norm_one, inverse_one = zip(*[normalize(own_tokens[slot]) for slot in each])
    norm_one_all = [gather_rows(norm_one[slot].astype(low), SEQUENCE_ROWS) for slot in each]

    attention_part, *ffn_grad = lax.optimization_barrier((attention_part, *ffn_grad))
    attention_w = gather_groups(attention_part)
    qkv_w, out_w = attention_w[:, : 3 * head_cols], attention_w[:, 3 * head_cols :]
    norm_one_all[0], ffn_block = lax.optimization_barrier((norm_one_all[0], ffn_block))
    hops = relay_hops(ffn_block)
    last = slots - 1
    ffn_grad_all = [gather_rows(ffn_grad[slot], PLANE_ROWS) for slot in each]

    def attend(slot):
        qkv = dot(norm_one_all[slot], qkv_w, ((1,), (0,)))
        query, key, value = (qkv[:, i * head_cols : (i + 1) * head_cols] for i in range(3))
        query = rotate(split(query), rope_cos, rope_sin).astype(low)
        key = rotate(split(key), rope_cos, rope_sin).astype(low)
        value = split(value.astype(low))
        scores = einsum("qhd,khd->hqk", query, key) * scale
        masked = jnp.where(allowed[slot], scores, -1e30)
        row_top = jnp.max(masked, axis=-1, keepdims=True)
        exponent = jnp.where(allowed[slot], jnp.exp(masked - row_top), 0.0)
        probabilities = exponent / jnp.sum(exponent, axis=-1, keepdims=True)
        attended = einsum("hqk,khd->qhd", probabilities.astype(low), value)
        attended = attended.reshape(seq, heads * HEAD_DIM).astype(low)
        return query, key, value, probabilities, attended

    saved, branch = [], []
    for slot in each:
        kept = attend(slot)
        attended = kept[4]
        if slot == 0:
            attended, *ffn_grad_all = lax.optimization_barrier((attended, *ffn_grad_all))
            attended = hold(attended, hops, 0)
        if slot == last:
            attended = hold(attended, hops, 1)
        saved.append(kept[:4] + (attended,))
        branch.append(scatter_rows(dot(attended, out_w, ((1,), (1,))), SEQUENCE_ROWS))
    middle, norm_two, inverse_two, norm_two_all = [], [], [], []
    for slot in each:
        summed_branch = branch[slot]
        if slot == last:
            summed_branch = hold(summed_branch, hops, 2)
        middle.append(own_tokens[slot] + valid_rows[slot] * summed_branch)
        normed, inverse = normalize(middle[slot])
        norm_two.append(normed)
        inverse_two.append(inverse)
        norm_two_all.append(gather_rows(normed.astype(low), PLANE_ROWS))
    ffn_w = assemble(ffn_block, hops)
    gate_up_w, down_w = ffn_w[:, : 2 * units], ffn_w[:, 2 * units :]

    hidden, gate_up_grad, norm_two_grad = [], [], []
    for slot in each:
        gate_up = dot(norm_two_all[slot], gate_up_w, ((1,), (0,)))
        gate, upper = gate_up[:, :units], gate_up[:, units:]
        sigmoid = jax.nn.sigmoid(gate)
        silu = gate * sigmoid
        hidden.append((silu * upper).astype(low))
        hidden_grad = dot(ffn_grad_all[slot], down_w, ((1,), (0,)))
        gate_grad = (hidden_grad * upper * sigmoid * (1.0 + gate * (1.0 - sigmoid))).astype(low)
        upper_grad = (hidden_grad * silu).astype(low)
        gate_up_grad.append(jnp.concatenate([gate_grad, upper_grad], axis=1))
        norm_two_grad.append(scatter_plane(dot(gate_up_grad[slot], gate_up_w, ((1,), (1,)))))

    def over_slots(terms):
        total = terms[0]
        for other in terms[1:]:
            total = total + other
        return total.astype(low)

    down_sum = over_slots([dot(ffn_grad_all[slot], hidden[slot], ((0,), (0,))) for slot in each])
    gate_up_sum = over_slots([dot(norm_two_all[slot], gate_up_grad[slot], ((0,), (0,))) for slot in each])
    ffn_sum = Reduction([gate_up_sum, down_sum], groups, contexts)

    middle_grad, branch_grad_all = [], []
    for slot in each:
        upstream = norm_two_grad[slot]
        middle_grad.append(
            out_grad[slot] + normalize_back(norm_two[slot], inverse_two[slot], upstream)
        )
        branch_grad_all.append(
            gather_rows((valid_rows[slot] * middle_grad[slot]).astype(low), SEQUENCE_ROWS)
        )
    branch_grad_all[0], *ffn_sum.parts = lax.optimization_barrier((branch_grad_all[0], *ffn_sum.parts))
    ffn_sum.hop()

    qkv_grad, norm_one_grad = [], []
    for slot in each:
        query, key, value, probabilities, attended = saved[slot]
        attended_grad = dot(branch_grad_all[slot], out_w, ((1,), (0,))).astype(low)
        if slot == last:
            attended_grad = ffn_sum.hold(attended_grad)
        attended_grad = split(attended_grad)
        prob_grad = einsum("qhd,khd->hqk", attended_grad, value)
        row_delta = jnp.sum(probabilities * prob_grad, axis=-1, keepdims=True)
        score_grad = (probabilities * (prob_grad - row_delta)).astype(low)
        query_grad = einsum("hqk,khd->qhd", score_grad, key) * scale
        key_grad = einsum("hqk,qhd->khd", score_grad, query) * scale
        value_grad = einsum("hqk,qhd->khd", probabilities.astype(low), attended_grad)
        qkv_grad.append(
            jnp.concatenate(
                [
                    unrotate(query_grad, rope_cos, rope_sin).astype(low).reshape(seq, -1),
                    unrotate(key_grad, rope_cos, rope_sin).astype(low).reshape(seq, -1),
                    value_grad.astype(low).reshape(seq, -1),
                ],
                axis=1,
            )
        )
        part = dot(qkv_grad[slot], qkv_w, ((1,), (1,))).astype(low)
        if slot + 1 < slots:
            part, branch_grad_all[slot + 1] = lax.optimization_barrier((part, branch_grad_all[slot + 1]))
        if slot + 1 == last:
            branch_grad_all[last], *hidden_late = lax.optimization_barrier(
                (branch_grad_all[last], *hidden)
            )
        norm_one_grad.append(scatter_rows(part, SEQUENCE_ROWS))
    out_sum = over_slots([dot(branch_grad_all[slot], saved[slot][4], ((0,), (0,))) for slot in each])
    qkv_sum = over_slots([dot(norm_one_all[slot], qkv_grad[slot], ((0,), (0,))) for slot in each])

    ffn_sum.hop()
    qkv_sum, norm_one_grad[0] = lax.optimization_barrier((qkv_sum, norm_one_grad[0]))
    qkv_sum = ffn_sum.hold(qkv_sum)

    layer_out, input_grad = [], []
    for slot in each:
        feedforward = scatter_plane(dot(hidden_late[slot], down_w, ((1,), (1,))))
        layer_out.append((middle[slot] + valid_rows[slot] * feedforward).astype(low))
    ffn_sum.hop()
    norm_one_grad[0], *layer_out = lax.optimization_barrier((norm_one_grad[0], *layer_out))
    attention_total = ffn_sum.hold(reduce_groups([qkv_sum, out_sum]))
    for slot in each:
        upstream = norm_one_grad[slot]
        input_grad.append(
            middle_grad[slot] + normalize_back(norm_one[slot], inverse_one[slot], upstream)
        )
    layer_out, input_grad = join_cores(jnp.stack(layer_out)), join_cores(jnp.stack(input_grad))

    ffn_pieces = ffn_sum.finish()
    attention_pieces = swap(attention_total.reshape(contexts, -1, 4 * head_cols), "context")

    def column_output(pieces, axis, start, size):
        members, here = lax.axis_size(axis), lax.axis_index(axis)
        whole = jnp.zeros((pieces[0].shape[0], members * size), jnp.float32)
        for step, piece in enumerate(pieces):
            block = piece[:, start : start + size].astype(jnp.float32)
            whole = lax.dynamic_update_slice_in_dim(whole, block, (here ^ step) * size, 1)
        return whole

    def row_output(pieces, axis, start, size):
        members, here = lax.axis_size(axis), lax.axis_index(axis)
        whole = jnp.zeros((members * size, pieces[0].shape[0]), jnp.float32)
        for step, piece in enumerate(pieces):
            block = piece[:, start : start + size].astype(jnp.float32).T
            whole = lax.dynamic_update_slice_in_dim(whole, block, (here ^ step) * size, 0)
        return whole

    grads = tuple(column_output(attention_pieces, "context", i * head_cols, head_cols) for i in range(3)) + (
        row_output(attention_pieces, "context", 3 * head_cols, head_cols),
        column_output(ffn_pieces, "dp", 0, units),
        column_output(ffn_pieces, "dp", units, units),
        row_output(ffn_pieces, "dp", 2 * units, units),
    )
    return (layer_out, input_grad) + grads


def solution(mesh):
    tokens = P("dp", "context", None)
    column = P(("dp", "context"), "tensor")
    row = P("tensor", ("dp", "context"))
    weights = (column, column, column, row, column, column, row)
    return jax.shard_map(
        per_device,
        mesh=mesh,
        in_specs=(tokens, P("dp")) + weights + (tokens,),
        out_specs=(tokens, tokens) + weights,
        check_vma=False,
    )
```

```python
import math

import jax
import jax.numpy as jnp
from jax import lax
from jax.sharding import PartitionSpec as P

HEAD_DIM = 128
SEQUENCE_ROWS = ("context", "tensor")
PLANE_ROWS = ("dp", "tensor")


def rope_tables(positions, head_dim):
    half_dim = head_dim // 2
    inverse_freq = jnp.exp(
        -math.log(10000.0) * jnp.arange(half_dim, dtype=jnp.float32) * 2.0 / head_dim
    )
    angles = positions.astype(jnp.float32)[:, None] * inverse_freq[None, :]
    angles = jnp.concatenate([angles, angles], axis=-1)
    return (jnp.cos(angles)[:, None, :], jnp.sin(angles)[:, None, :])


def rotate(values, cosine, sine):
    half_dim = values.shape[-1] // 2
    turned = jnp.concatenate([-values[..., half_dim:], values[..., :half_dim]], axis=-1)
    return values * cosine + turned * sine


def unrotate(upstream, cosine, sine):
    half_dim = upstream.shape[-1] // 2
    scaled = upstream * sine
    turned = jnp.concatenate([scaled[..., half_dim:], -scaled[..., :half_dim]], axis=-1)
    return upstream * cosine + turned


def normalize(values):
    centered = values - jnp.mean(values, axis=-1, keepdims=True)
    inverse = lax.rsqrt(jnp.mean(centered * centered, axis=-1, keepdims=True) + 1e-05)
    return (centered * inverse, inverse)


def normalize_back(normed, inverse, upstream):
    mean_grad = jnp.mean(upstream, axis=-1, keepdims=True)
    mean_cross = jnp.mean(upstream * normed, axis=-1, keepdims=True)
    return inverse * (upstream - mean_grad - normed * mean_cross)


def dot(left, right, dims):
    return lax.dot_general(left, right, (dims, ((), ())), preferred_element_type=jnp.float32)


def gather_rows(values, axes):
    return lax.all_gather(values, axes, axis=0, tiled=True)


def scatter_rows(values, axes):
    return lax.psum_scatter(values.astype(jnp.bfloat16), axes, scatter_dimension=0, tiled=True).astype(
        jnp.float32
    )


def join_cores(values):
    cores = lax.axis_size("tensor")
    core, rows = lax.axis_index("tensor"), values.shape[1]
    whole = jnp.concatenate([values] * cores, axis=1)
    for step in range(1, cores):
        route = [(i, (i + step) % cores) for i in range(cores)]
        other = lax.ppermute(values, "tensor", route)
        whole = lax.dynamic_update_slice_in_dim(whole, other, ((core - step) % cores) * rows, 1)
    return whole


def put(buffer, piece, index):
    return lax.dynamic_update_slice_in_dim(buffer, piece[None], index, 0)


def take(buffer, index):
    return lax.dynamic_index_in_dim(buffer, index, 0, keepdims=False)


def trade(weight, axis):
    return exchange(jnp.moveaxis(weight, 1, 0), axis)


def gather_groups(mine):
    group, groups = lax.axis_index("dp"), lax.axis_size("dp")
    whole = jnp.zeros((groups,) + mine.shape, mine.dtype)
    whole = put(whole, mine, group)
    for step in range(1, groups):
        route = [(i, i ^ step) for i in range(groups)]
        whole = put(whole, lax.ppermute(mine, "dp", route), group ^ step)
    return whole.reshape(-1, mine.shape[-1])


def reduce_groups(partials):
    group, groups = lax.axis_index("dp"), lax.axis_size("dp")
    parts = [partial.reshape(groups, -1, partial.shape[1]) for partial in partials]

    def term(index):
        return jnp.concatenate([take(part, index) for part in parts], axis=1)

    total = term(group).astype(jnp.float32)
    for step in range(1, groups):
        route = [(i, i ^ step) for i in range(groups)]
        total = total + lax.ppermute(term(group ^ step), "dp", route).astype(jnp.float32)
    return total.astype(jnp.bfloat16)


def swap(pieces, axis):
    members, here = lax.axis_size(axis), lax.axis_index(axis)
    arrived = [take(pieces, here)]
    for step in range(1, members):
        route = [(i, i ^ step) for i in range(members)]
        arrived.append(lax.ppermute(take(pieces, here ^ step), axis, route))
    return arrived


def exchange(pieces, axis):
    here = lax.axis_index(axis)
    mine = jnp.zeros_like(pieces)
    for step, piece in enumerate(swap(pieces, axis)):
        mine = put(mine, piece, here ^ step)
    return mine


def relay_hops(block):
    n = lax.axis_size("context")
    up, down = [], []
    moving_up = moving_down = block
    for step in range(1, n):
        moving_up = lax.ppermute(moving_up, "context", [(i, i + 1) for i in range(step - 1, n - 1)])
        moving_down = lax.ppermute(moving_down, "context", [(i, i - 1) for i in range(1, n - step + 1)])
        up.append(moving_up)
        down.append(moving_down)
    return up, down


def hold(value, hops, index):
    up, down = hops
    if index < len(up):
        value, up[index], down[index] = lax.optimization_barrier((value, up[index], down[index]))
    return value


def assemble(block, hops):
    n, here = lax.axis_size("context"), lax.axis_index("context")
    up, down = hops
    groups, rows, columns = block.shape
    whole = jnp.zeros((groups, n, rows, columns), block.dtype)
    whole = lax.dynamic_update_slice_in_dim(whole, block[:, None], here, 1)
    for step in range(1, n):
        piece = jnp.where(here >= step, up[step - 1], down[n - step - 1])
        whole = lax.dynamic_update_slice_in_dim(whole, piece[:, None], (here - step) % n, 1)
    return whole.reshape(-1, columns)


def scatter_plane(values):
    low = jnp.bfloat16
    cores, groups = lax.axis_size("tensor"), lax.axis_size("dp")
    core, group = lax.axis_index("tensor"), lax.axis_index("dp")
    width = values.shape[1]
    parts = values.astype(low).reshape(groups, cores, -1, width)

    def of_core(index):
        return lax.dynamic_index_in_dim(parts, index % cores, 1, keepdims=False)

    total = of_core(core).astype(jnp.float32)
    for step in range(1, cores):
        route = [(i, (i + step) % cores) for i in range(cores)]
        total = total + lax.ppermute(of_core(core + step), "tensor", route).astype(jnp.float32)
    total = total.astype(low)
    bits = list(range(groups.bit_length() - 1))
    results = []
    for part, order in enumerate((bits, bits[::-1])):
        half = width // 2
        block = total[:, :, part * half : (part + 1) * half]
        rows = block.shape[1]
        block = block.reshape((2,) * len(bits) + (rows, half))
        left = bits[::-1]
        for bit in order:
            axis, mine = left.index(bit), (group >> bit) & 1
            keep = lax.dynamic_index_in_dim(block, mine, axis, keepdims=False)
            send = lax.dynamic_index_in_dim(block, 1 - mine, axis, keepdims=False)
            route = [(i, i ^ (1 << bit)) for i in range(groups)]
            other = lax.ppermute(send, "dp", route)
            block = keep.astype(jnp.float32) + other.astype(jnp.float32)
            left.remove(bit)
            if left:
                block = block.astype(low)
        results.append(block)
    return jnp.concatenate(results, axis=1)


class Reduction:
    def __init__(self, partials, groups, contexts):
        self.parts = [partial.reshape(groups, contexts, -1, partial.shape[1]) for partial in partials]
        self.n, self.here = contexts, lax.axis_index("context")
        self.above = self.below = None
        self.step = 0

    def term(self, index):
        picked = [lax.dynamic_index_in_dim(part, index % self.n, 1, keepdims=False) for part in self.parts]
        return jnp.concatenate(picked, axis=-1).astype(jnp.float32)

    def hop(self):
        if self.step == self.n - 1:
            return
        self.step += 1
        step, n = self.step, self.n
        above, below = self.term(self.here - step), self.term(self.here + step)
        if self.above is not None:
            above, below = above + self.above.astype(jnp.float32), below + self.below.astype(jnp.float32)
        self.above = lax.ppermute(
            above.astype(jnp.bfloat16), "context", [(i, i + 1) for i in range(min(step, n - 1))]
        )
        self.below = lax.ppermute(
            below.astype(jnp.bfloat16), "context", [(i, i - 1) for i in range(max(1, n - step), n)]
        )

    def hold(self, value):
        value, self.above, self.below = lax.optimization_barrier((value, self.above, self.below))
        return value

    def finish(self):
        while self.step < self.n - 1:
            self.hop()
        total = self.term(self.here) + self.above.astype(jnp.float32) + self.below.astype(jnp.float32)
        return swap(total.astype(jnp.bfloat16), "dp")


def per_device(tokens, lengths, w_query, w_key, w_value, w_out, w_gate, w_up, w_down, cotangent):
    low = jnp.bfloat16
    slots, chip_rows, width = tokens.shape
    contexts, cores = lax.axis_size("context"), lax.axis_size("tensor")
    rows = chip_rows // cores
    seq = chip_rows * contexts
    head_cols = w_query.shape[1] // contexts
    groups = lax.axis_size("dp")
    units = w_gate.shape[1] // groups
    heads = head_cols // HEAD_DIM
    scale = 1.0 / math.sqrt(HEAD_DIM)
    core = lax.axis_index("tensor")
    own_start = lax.axis_index("context") * chip_rows + core * rows
    own_positions = own_start + jnp.arange(rows, dtype=jnp.int32)
    positions = jnp.arange(seq, dtype=jnp.int32)
    rope_cos, rope_sin = rope_tables(positions, HEAD_DIM)
    causal = positions[None, :] <= positions[:, None]

    def by_context(weight):
        return weight.reshape(weight.shape[0], contexts, -1)

    attention_part = trade(
        jnp.concatenate([by_context(w) for w in (w_query, w_key, w_value, w_out.T)], axis=2), "context"
    )

    def by_group(weight):
        return jnp.moveaxis(weight.reshape(weight.shape[0], groups, -1), 1, 0)

    ffn_block = exchange(
        jnp.concatenate([by_group(w) for w in (w_gate, w_up, w_down.T)], axis=2), "dp"
    )

    def einsum(form, left, right):
        return jnp.einsum(form, left, right, preferred_element_type=jnp.float32)

    def split(values):
        return values.reshape(seq, heads, HEAD_DIM)

    def own(array, slot):
        return lax.dynamic_slice_in_dim(array[slot], core * rows, rows, 0).astype(jnp.float32)

    each = range(slots)
    own_tokens = [own(tokens, slot) for slot in each]
    valid_rows = [(own_positions < lengths[slot]).astype(jnp.float32)[:, None] for slot in each]
    allowed = [(causal & (positions < lengths[slot])[None, :])[None] for slot in each]
    out_grad = [own(cotangent, slot) * valid_rows[slot] for slot in each]
    ffn_grad = [(valid_rows[slot] * out_grad[slot]).astype(low) for slot in each]
    norm_one, inverse_one = zip(*[normalize(own_tokens[slot]) for slot in each])
    norm_one_all = [gather_rows(norm_one[slot].astype(low), SEQUENCE_ROWS) for slot in each]

    attention_part, ffn_block, *ffn_grad = lax.optimization_barrier(
        (attention_part, ffn_block, *ffn_grad)
    )
    attention_w = gather_groups(attention_part)
    qkv_w, out_w = attention_w[:, : 3 * head_cols], attention_w[:, 3 * head_cols :]
    hops = relay_hops(ffn_block)
    last = slots - 1
    ffn_grad_all = [gather_rows(ffn_grad[slot], PLANE_ROWS) for slot in each]

    def attend(slot):
        qkv = dot(norm_one_all[slot], qkv_w, ((1,), (0,)))
        if slot + 1 < slots:
            qkv, norm_one_all[slot + 1] = lax.optimization_barrier((qkv, norm_one_all[slot + 1]))
        if slot + 1 == last:
            norm_one_all[last] = hold(norm_one_all[last], hops, 0)
        query, key, value = (qkv[:, i * head_cols : (i + 1) * head_cols] for i in range(3))
        query = rotate(split(query), rope_cos, rope_sin).astype(low)
        key = rotate(split(key), rope_cos, rope_sin).astype(low)
        value = split(value.astype(low))
        scores = einsum("qhd,khd->hqk", query, key) * scale
        masked = jnp.where(allowed[slot], scores, -1e30)
        row_top = jnp.max(masked, axis=-1, keepdims=True)
        exponent = jnp.where(allowed[slot], jnp.exp(masked - row_top), 0.0)
        probabilities = exponent / jnp.sum(exponent, axis=-1, keepdims=True)
        attended = einsum("hqk,khd->qhd", probabilities.astype(low), value)
        attended = attended.reshape(seq, heads * HEAD_DIM).astype(low)
        return query, key, value, probabilities, attended

    saved = [attend(slot) for slot in each]
    attended = [kept[4] for kept in saved]
    branch = []
    for slot in each:
        if slot == last:
            attended[slot], *ffn_grad_all = lax.optimization_barrier((attended[slot], *ffn_grad_all))
        part = dot(attended[slot], out_w, ((1,), (1,))).astype(low)
        if slot + 1 < slots:
            part, attended[slot + 1] = lax.optimization_barrier((part, attended[slot + 1]))
        if slot == 0:
            part = hold(part, hops, 1)
        branch.append(scatter_rows(part, SEQUENCE_ROWS))
    middle, norm_two, inverse_two, norm_two_all = [], [], [], []
    for slot in each:
        summed_branch = branch[slot]
        if slot == 0:
            summed_branch = hold(summed_branch, hops, 2)
        middle.append(own_tokens[slot] + valid_rows[slot] * summed_branch)
        normed, inverse = normalize(middle[slot])
        norm_two.append(normed)
        inverse_two.append(inverse)
        norm_two_all.append(gather_rows(normed.astype(low), PLANE_ROWS))
    ffn_w = assemble(ffn_block, hops)
    gate_up_w, down_w = ffn_w[:, : 2 * units], ffn_w[:, 2 * units :]

    hidden, gate_up_grad, norm_two_grad = [], [], []
    for slot in each:
        gate_up = dot(norm_two_all[slot], gate_up_w, ((1,), (0,)))
        gate, upper = gate_up[:, :units], gate_up[:, units:]
        sigmoid = jax.nn.sigmoid(gate)
        silu = gate * sigmoid
        hidden.append((silu * upper).astype(low))
        hidden_grad = dot(ffn_grad_all[slot], down_w, ((1,), (0,)))
        gate_grad = (hidden_grad * upper * sigmoid * (1.0 + gate * (1.0 - sigmoid))).astype(low)
        upper_grad = (hidden_grad * silu).astype(low)
        gate_up_grad.append(jnp.concatenate([gate_grad, upper_grad], axis=1))
        norm_two_grad.append(dot(gate_up_grad[slot], gate_up_w, ((1,), (1,))).astype(low))

    def over_slots(terms):
        total = terms[0]
        for other in terms[1:]:
            total = total + other
        return total.astype(low)

    down_sum = over_slots([dot(ffn_grad_all[slot], hidden[slot], ((0,), (0,))) for slot in each])
    gate_up_sum = over_slots([dot(norm_two_all[slot], gate_up_grad[slot], ((0,), (0,))) for slot in each])
    norm_two_grad[last], gate_up_sum, down_sum = lax.optimization_barrier(
        (norm_two_grad[last], gate_up_sum, down_sum)
    )
    norm_two_grad = [scatter_plane(norm_two_grad[slot]) for slot in each]
    ffn_sum = Reduction([gate_up_sum, down_sum], groups, contexts)

    middle_grad, branch_grad_all = [], []
    for slot in each:
        upstream = norm_two_grad[slot]
        middle_grad.append(
            out_grad[slot] + normalize_back(norm_two[slot], inverse_two[slot], upstream)
        )
        branch_grad_all.append(
            gather_rows((valid_rows[slot] * middle_grad[slot]).astype(low), SEQUENCE_ROWS)
        )
    ffn_sum.hop()

    qkv_grad, norm_one_grad = [], []
    for slot in each:
        query, key, value, probabilities, _ = saved[slot]
        attended_grad = dot(branch_grad_all[slot], out_w, ((1,), (0,))).astype(low)
        attended_grad = split(attended_grad)
        prob_grad = einsum("qhd,khd->hqk", attended_grad, value)
        row_delta = jnp.sum(probabilities * prob_grad, axis=-1, keepdims=True)
        score_grad = (probabilities * (prob_grad - row_delta)).astype(low)
        query_grad = einsum("hqk,khd->qhd", score_grad, key) * scale
        key_grad = einsum("hqk,qhd->khd", score_grad, query) * scale
        value_grad = einsum("hqk,qhd->khd", probabilities.astype(low), attended_grad)
        qkv_grad.append(
            jnp.concatenate(
                [
                    unrotate(query_grad, rope_cos, rope_sin).astype(low).reshape(seq, -1),
                    unrotate(key_grad, rope_cos, rope_sin).astype(low).reshape(seq, -1),
                    value_grad.astype(low).reshape(seq, -1),
                ],
                axis=1,
            )
        )
        part = dot(qkv_grad[slot], qkv_w, ((1,), (1,))).astype(low)
        if slot + 1 == last:
            part = ffn_sum.hold(part)
        if slot + 1 < slots:
            part, branch_grad_all[slot + 1] = lax.optimization_barrier((part, branch_grad_all[slot + 1]))
        if slot + 1 == last:
            branch_grad_all[last], *hidden_late = lax.optimization_barrier(
                (branch_grad_all[last], *hidden)
            )
        norm_one_grad.append(scatter_rows(part, SEQUENCE_ROWS))
    out_sum = over_slots([dot(branch_grad_all[slot], attended[slot], ((0,), (0,))) for slot in each])
    qkv_sum = over_slots([dot(norm_one_all[slot], qkv_grad[slot], ((0,), (0,))) for slot in each])

    ffn_sum.hop()
    qkv_sum, norm_one_grad[0] = lax.optimization_barrier((qkv_sum, norm_one_grad[0]))
    qkv_sum = ffn_sum.hold(qkv_sum)

    layer_out, input_grad = [], []
    for slot in each:
        feedforward = scatter_plane(dot(hidden_late[slot], down_w, ((1,), (1,))))
        layer_out.append((middle[slot] + valid_rows[slot] * feedforward).astype(low))
    ffn_sum.hop()
    norm_one_grad[0], *layer_out = lax.optimization_barrier((norm_one_grad[0], *layer_out))
    attention_total = ffn_sum.hold(reduce_groups([qkv_sum, out_sum]))
    for slot in each:
        upstream = norm_one_grad[slot]
        input_grad.append(
            middle_grad[slot] + normalize_back(norm_one[slot], inverse_one[slot], upstream)
        )
    layer_out, input_grad = join_cores(jnp.stack(layer_out)), join_cores(jnp.stack(input_grad))

    ffn_pieces = ffn_sum.finish()
    attention_pieces = swap(attention_total.reshape(contexts, -1, 4 * head_cols), "context")

    def column_output(pieces, axis, start, size):
        members, here = lax.axis_size(axis), lax.axis_index(axis)
        whole = jnp.zeros((pieces[0].shape[0], members * size), jnp.float32)
        for step, piece in enumerate(pieces):
            block = piece[:, start : start + size].astype(jnp.float32)
            whole = lax.dynamic_update_slice_in_dim(whole, block, (here ^ step) * size, 1)
        return whole

    def row_output(pieces, axis, start, size):
        members, here = lax.axis_size(axis), lax.axis_index(axis)
        whole = jnp.zeros((members * size, pieces[0].shape[0]), jnp.float32)
        for step, piece in enumerate(pieces):
            block = piece[:, start : start + size].astype(jnp.float32).T
            whole = lax.dynamic_update_slice_in_dim(whole, block, (here ^ step) * size, 0)
        return whole

    grads = tuple(column_output(attention_pieces, "context", i * head_cols, head_cols) for i in range(3)) + (
        row_output(attention_pieces, "context", 3 * head_cols, head_cols),
        column_output(ffn_pieces, "dp", 0, units),
        column_output(ffn_pieces, "dp", units, units),
        row_output(ffn_pieces, "dp", 2 * units, units),
    )
    return (layer_out, input_grad) + grads


def solution(mesh):
    tokens = P("dp", "context", None)
    column = P(("dp", "context"), "tensor")
    row = P("tensor", ("dp", "context"))
    weights = (column, column, column, row, column, column, row)
    return jax.shard_map(
        per_device,
        mesh=mesh,
        in_specs=(tokens, P("dp")) + weights + (tokens,),
        out_specs=(tokens, tokens) + weights,
        check_vma=False,
    )
```

```python
import math

import jax
import jax.numpy as jnp
from jax import lax
from jax.sharding import PartitionSpec as P

HEAD_DIM = 128
SEQUENCE_ROWS = ("context", "tensor")
PLANE_ROWS = ("dp", "tensor")


def rope_tables(positions, head_dim):
    half_dim = head_dim // 2
    inverse_freq = jnp.exp(
        -math.log(10000.0) * jnp.arange(half_dim, dtype=jnp.float32) * 2.0 / head_dim
    )
    angles = positions.astype(jnp.float32)[:, None] * inverse_freq[None, :]
    angles = jnp.concatenate([angles, angles], axis=-1)
    return (jnp.cos(angles)[:, None, :], jnp.sin(angles)[:, None, :])


def rotate(values, cosine, sine):
    half_dim = values.shape[-1] // 2
    turned = jnp.concatenate([-values[..., half_dim:], values[..., :half_dim]], axis=-1)
    return values * cosine + turned * sine


def unrotate(upstream, cosine, sine):
    half_dim = upstream.shape[-1] // 2
    scaled = upstream * sine
    turned = jnp.concatenate([scaled[..., half_dim:], -scaled[..., :half_dim]], axis=-1)
    return upstream * cosine + turned


def normalize(values):
    centered = values - jnp.mean(values, axis=-1, keepdims=True)
    inverse = lax.rsqrt(jnp.mean(centered * centered, axis=-1, keepdims=True) + 1e-05)
    return (centered * inverse, inverse)


def normalize_back(normed, inverse, upstream):
    mean_grad = jnp.mean(upstream, axis=-1, keepdims=True)
    mean_cross = jnp.mean(upstream * normed, axis=-1, keepdims=True)
    return inverse * (upstream - mean_grad - normed * mean_cross)


def dot(left, right, dims):
    return lax.dot_general(left, right, (dims, ((), ())), preferred_element_type=jnp.float32)


def gather_rows(values, axes):
    return lax.all_gather(values, axes, axis=0, tiled=True)


def scatter_rows(values, axes):
    return lax.psum_scatter(values.astype(jnp.bfloat16), axes, scatter_dimension=0, tiled=True).astype(
        jnp.float32
    )


def join_cores(values):
    cores = lax.axis_size("tensor")
    core, rows = lax.axis_index("tensor"), values.shape[1]
    whole = jnp.concatenate([values] * cores, axis=1)
    for step in range(1, cores):
        route = [(i, (i + step) % cores) for i in range(cores)]
        other = lax.ppermute(values, "tensor", route)
        whole = lax.dynamic_update_slice_in_dim(whole, other, ((core - step) % cores) * rows, 1)
    return whole


def put(buffer, piece, index):
    return lax.dynamic_update_slice_in_dim(buffer, piece[None], index, 0)


def take(buffer, index):
    return lax.dynamic_index_in_dim(buffer, index, 0, keepdims=False)


def trade(weight, axis):
    return exchange(jnp.moveaxis(weight, 1, 0), axis)


def gather_groups(mine):
    group, groups = lax.axis_index("dp"), lax.axis_size("dp")
    whole = jnp.zeros((groups,) + mine.shape, mine.dtype)
    whole = put(whole, mine, group)
    for step in range(1, groups):
        route = [(i, i ^ step) for i in range(groups)]
        whole = put(whole, lax.ppermute(mine, "dp", route), group ^ step)
    return whole.reshape(-1, mine.shape[-1])


def reduce_groups(partials):
    group, groups = lax.axis_index("dp"), lax.axis_size("dp")
    parts = [partial.reshape(groups, -1, partial.shape[1]) for partial in partials]

    def term(index):
        return jnp.concatenate([take(part, index) for part in parts], axis=1)

    total = term(group).astype(jnp.float32)
    for step in range(1, groups):
        route = [(i, i ^ step) for i in range(groups)]
        total = total + lax.ppermute(term(group ^ step), "dp", route).astype(jnp.float32)
    return total.astype(jnp.bfloat16)


def swap(pieces, axis):
    members, here = lax.axis_size(axis), lax.axis_index(axis)
    arrived = [take(pieces, here)]
    for step in range(1, members):
        route = [(i, i ^ step) for i in range(members)]
        arrived.append(lax.ppermute(take(pieces, here ^ step), axis, route))
    return arrived


def exchange(pieces, axis):
    here = lax.axis_index(axis)
    mine = jnp.zeros_like(pieces)
    for step, piece in enumerate(swap(pieces, axis)):
        mine = put(mine, piece, here ^ step)
    return mine


def relay_hops(block):
    n = lax.axis_size("context")
    up, down = [], []
    moving_up = moving_down = block
    for step in range(1, n):
        moving_up = lax.ppermute(moving_up, "context", [(i, i + 1) for i in range(step - 1, n - 1)])
        moving_down = lax.ppermute(moving_down, "context", [(i, i - 1) for i in range(1, n - step + 1)])
        up.append(moving_up)
        down.append(moving_down)
    return up, down


def hold(value, hops, index):
    up, down = hops
    if index < len(up):
        value, up[index], down[index] = lax.optimization_barrier((value, up[index], down[index]))
    return value


def assemble(block, hops):
    n, here = lax.axis_size("context"), lax.axis_index("context")
    up, down = hops
    groups, rows, columns = block.shape
    whole = jnp.zeros((groups, n, rows, columns), block.dtype)
    whole = lax.dynamic_update_slice_in_dim(whole, block[:, None], here, 1)
    for step in range(1, n):
        piece = jnp.where(here >= step, up[step - 1], down[n - step - 1])
        whole = lax.dynamic_update_slice_in_dim(whole, piece[:, None], (here - step) % n, 1)
    return whole.reshape(-1, columns)


def scatter_plane(values):
    low = jnp.bfloat16
    cores, groups = lax.axis_size("tensor"), lax.axis_size("dp")
    core, group = lax.axis_index("tensor"), lax.axis_index("dp")
    width = values.shape[1]
    parts = values.astype(low).reshape(groups, cores, -1, width)

    def of_core(index):
        return lax.dynamic_index_in_dim(parts, index % cores, 1, keepdims=False)

    total = of_core(core).astype(jnp.float32)
    for step in range(1, cores):
        route = [(i, (i + step) % cores) for i in range(cores)]
        total = total + lax.ppermute(of_core(core + step), "tensor", route).astype(jnp.float32)
    total = total.astype(low)
    bits = list(range(groups.bit_length() - 1))
    results = []
    for part, order in enumerate((bits, bits[::-1])):
        half = width // 2
        block = total[:, :, part * half : (part + 1) * half]
        rows = block.shape[1]
        block = block.reshape((2,) * len(bits) + (rows, half))
        left = bits[::-1]
        for bit in order:
            axis, mine = left.index(bit), (group >> bit) & 1
            keep = lax.dynamic_index_in_dim(block, mine, axis, keepdims=False)
            send = lax.dynamic_index_in_dim(block, 1 - mine, axis, keepdims=False)
            route = [(i, i ^ (1 << bit)) for i in range(groups)]
            other = lax.ppermute(send, "dp", route)
            block = keep.astype(jnp.float32) + other.astype(jnp.float32)
            left.remove(bit)
            if left:
                block = block.astype(low)
        results.append(block)
    return jnp.concatenate(results, axis=1)


class Reduction:
    def __init__(self, partials, groups, contexts):
        self.parts = [partial.reshape(groups, contexts, -1, partial.shape[1]) for partial in partials]
        self.n, self.here = contexts, lax.axis_index("context")
        self.above = self.below = None
        self.step = 0

    def term(self, index):
        picked = [lax.dynamic_index_in_dim(part, index % self.n, 1, keepdims=False) for part in self.parts]
        return jnp.concatenate(picked, axis=-1).astype(jnp.float32)

    def hop(self):
        if self.step == self.n - 1:
            return
        self.step += 1
        step, n = self.step, self.n
        above, below = self.term(self.here - step), self.term(self.here + step)
        if self.above is not None:
            above, below = above + self.above.astype(jnp.float32), below + self.below.astype(jnp.float32)
        self.above = lax.ppermute(
            above.astype(jnp.bfloat16), "context", [(i, i + 1) for i in range(min(step, n - 1))]
        )
        self.below = lax.ppermute(
            below.astype(jnp.bfloat16), "context", [(i, i - 1) for i in range(max(1, n - step), n)]
        )

    def hold(self, value):
        value, self.above, self.below = lax.optimization_barrier((value, self.above, self.below))
        return value

    def finish(self):
        while self.step < self.n - 1:
            self.hop()
        total = self.term(self.here) + self.above.astype(jnp.float32) + self.below.astype(jnp.float32)
        return swap(total.astype(jnp.bfloat16), "dp")


def per_device(tokens, lengths, w_query, w_key, w_value, w_out, w_gate, w_up, w_down, cotangent):
    low = jnp.bfloat16
    slots, chip_rows, width = tokens.shape
    contexts, cores = lax.axis_size("context"), lax.axis_size("tensor")
    rows = chip_rows // cores
    seq = chip_rows * contexts
    head_cols = w_query.shape[1] // contexts
    groups = lax.axis_size("dp")
    units = w_gate.shape[1] // groups
    heads = head_cols // HEAD_DIM
    scale = 1.0 / math.sqrt(HEAD_DIM)
    core = lax.axis_index("tensor")
    own_start = lax.axis_index("context") * chip_rows + core * rows
    own_positions = own_start + jnp.arange(rows, dtype=jnp.int32)
    positions = jnp.arange(seq, dtype=jnp.int32)
    rope_cos, rope_sin = rope_tables(positions, HEAD_DIM)
    causal = positions[None, :] <= positions[:, None]

    def by_context(weight):
        return weight.reshape(weight.shape[0], contexts, -1)

    attention_part = trade(
        jnp.concatenate([by_context(w) for w in (w_query, w_key, w_value, w_out.T)], axis=2), "context"
    )

    def by_group(weight):
        return jnp.moveaxis(weight.reshape(weight.shape[0], groups, -1), 1, 0)

    ffn_block = exchange(
        jnp.concatenate([by_group(w) for w in (w_gate, w_up, w_down.T)], axis=2), "dp"
    )

    def einsum(form, left, right):
        return jnp.einsum(form, left, right, preferred_element_type=jnp.float32)

    def split(values):
        return values.reshape(seq, heads, HEAD_DIM)

    def own(array, slot):
        return lax.dynamic_slice_in_dim(array[slot], core * rows, rows, 0).astype(jnp.float32)

    each = range(slots)
    own_tokens = [own(tokens, slot) for slot in each]
    valid_rows = [(own_positions < lengths[slot]).astype(jnp.float32)[:, None] for slot in each]
    allowed = [(causal & (positions < lengths[slot])[None, :])[None] for slot in each]
    out_grad = [own(cotangent, slot) * valid_rows[slot] for slot in each]
    ffn_grad = [(valid_rows[slot] * out_grad[slot]).astype(low) for slot in each]
    norm_one, inverse_one = zip(*[normalize(own_tokens[slot]) for slot in each])
    norm_one_all = [gather_rows(norm_one[slot].astype(low), SEQUENCE_ROWS) for slot in each]

    attention_part, ffn_block, *ffn_grad = lax.optimization_barrier(
        (attention_part, ffn_block, *ffn_grad)
    )
    attention_w = gather_groups(attention_part)
    qkv_w, out_w = attention_w[:, : 3 * head_cols], attention_w[:, 3 * head_cols :]
    hops = relay_hops(ffn_block)
    last = slots - 1
    ffn_grad_all = [gather_rows(ffn_grad[slot], PLANE_ROWS) for slot in each]

    def attend(slot):
        qkv = dot(norm_one_all[slot], qkv_w, ((1,), (0,)))
        if slot + 1 < slots:
            qkv, norm_one_all[slot + 1] = lax.optimization_barrier((qkv, norm_one_all[slot + 1]))
        if slot + 1 == last:
            norm_one_all[last] = hold(norm_one_all[last], hops, 0)
        query, key, value = (qkv[:, i * head_cols : (i + 1) * head_cols] for i in range(3))
        query = rotate(split(query), rope_cos, rope_sin).astype(low)
        key = rotate(split(key), rope_cos, rope_sin).astype(low)
        value = split(value.astype(low))
        scores = einsum("qhd,khd->hqk", query, key) * scale
        masked = jnp.where(allowed[slot], scores, -1e30)
        row_top = jnp.max(masked, axis=-1, keepdims=True)
        exponent = jnp.where(allowed[slot], jnp.exp(masked - row_top), 0.0)
        probabilities = exponent / jnp.sum(exponent, axis=-1, keepdims=True)
        attended = einsum("hqk,khd->qhd", probabilities.astype(low), value)
        attended = attended.reshape(seq, heads * HEAD_DIM).astype(low)
        return query, key, value, probabilities, attended

    saved = [attend(slot) for slot in each]
    attended = [kept[4] for kept in saved]
    branch = []
    for slot in each:
        if slot == last:
            attended[slot], *ffn_grad_all = lax.optimization_barrier((attended[slot], *ffn_grad_all))
        part = dot(attended[slot], out_w, ((1,), (1,))).astype(low)
        if slot + 1 < slots:
            part, attended[slot + 1] = lax.optimization_barrier((part, attended[slot + 1]))
        if slot == 0:
            part = hold(part, hops, 1)
        branch.append(scatter_rows(part, SEQUENCE_ROWS))
    middle, norm_two, inverse_two, norm_two_all = [], [], [], []
    for slot in each:
        summed_branch = branch[slot]
        if slot == 0:
            summed_branch = hold(summed_branch, hops, 2)
        middle.append(own_tokens[slot] + valid_rows[slot] * summed_branch)
        normed, inverse = normalize(middle[slot])
        norm_two.append(normed)
        inverse_two.append(inverse)
        norm_two_all.append(gather_rows(normed.astype(low), PLANE_ROWS))
    ffn_w = assemble(ffn_block, hops)
    gate_up_w, down_w = ffn_w[:, : 2 * units], ffn_w[:, 2 * units :]

    hidden, gate_up_grad, norm_two_grad = [], [], []
    for slot in each:
        gate_up = dot(norm_two_all[slot], gate_up_w, ((1,), (0,)))
        gate, upper = gate_up[:, :units], gate_up[:, units:]
        sigmoid = jax.nn.sigmoid(gate)
        silu = gate * sigmoid
        hidden.append((silu * upper).astype(low))
        hidden_grad = dot(ffn_grad_all[slot], down_w, ((1,), (0,)))
        gate_grad = (hidden_grad * upper * sigmoid * (1.0 + gate * (1.0 - sigmoid))).astype(low)
        upper_grad = (hidden_grad * silu).astype(low)
        gate_up_grad.append(jnp.concatenate([gate_grad, upper_grad], axis=1))
        norm_two_grad.append(dot(gate_up_grad[slot], gate_up_w, ((1,), (1,))).astype(low))

    def over_slots(terms):
        total = terms[0]
        for other in terms[1:]:
            total = total + other
        return total.astype(low)

    down_sum = over_slots([dot(ffn_grad_all[slot], hidden[slot], ((0,), (0,))) for slot in each])
    gate_up_sum = over_slots([dot(norm_two_all[slot], gate_up_grad[slot], ((0,), (0,))) for slot in each])
    norm_two_grad[last], gate_up_sum, down_sum = lax.optimization_barrier(
        (norm_two_grad[last], gate_up_sum, down_sum)
    )
    norm_two_grad = [scatter_plane(norm_two_grad[slot]) for slot in each]
    ffn_sum = Reduction([gate_up_sum, down_sum], groups, contexts)

    middle_grad, branch_grad_all = [], []
    for slot in each:
        upstream = norm_two_grad[slot]
        middle_grad.append(
            out_grad[slot] + normalize_back(norm_two[slot], inverse_two[slot], upstream)
        )
        branch_grad_all.append(
            gather_rows((valid_rows[slot] * middle_grad[slot]).astype(low), SEQUENCE_ROWS)
        )
    ffn_sum.hop()

    qkv_grad, norm_one_grad = [], []
    for slot in each:
        query, key, value, probabilities, _ = saved[slot]
        attended_grad = dot(branch_grad_all[slot], out_w, ((1,), (0,))).astype(low)
        attended_grad = split(attended_grad)
        prob_grad = einsum("qhd,khd->hqk", attended_grad, value)
        row_delta = jnp.sum(probabilities * prob_grad, axis=-1, keepdims=True)
        score_grad = (probabilities * (prob_grad - row_delta)).astype(low)
        query_grad = einsum("hqk,khd->qhd", score_grad, key) * scale
        key_grad = einsum("hqk,qhd->khd", score_grad, query) * scale
        value_grad = einsum("hqk,qhd->khd", probabilities.astype(low), attended_grad)
        qkv_grad.append(
            jnp.concatenate(
                [
                    unrotate(query_grad, rope_cos, rope_sin).astype(low).reshape(seq, -1),
                    unrotate(key_grad, rope_cos, rope_sin).astype(low).reshape(seq, -1),
                    value_grad.astype(low).reshape(seq, -1),
                ],
                axis=1,
            )
        )
        part = dot(qkv_grad[slot], qkv_w, ((1,), (1,))).astype(low)
        if slot == last:
            ffn_sum.hop()
        if slot + 1 >= last:
            part = ffn_sum.hold(part)
        if slot + 1 < slots:
            part, branch_grad_all[slot + 1] = lax.optimization_barrier((part, branch_grad_all[slot + 1]))
        norm_one_grad.append(scatter_rows(part, SEQUENCE_ROWS))
    out_sum = over_slots([dot(branch_grad_all[slot], attended[slot], ((0,), (0,))) for slot in each])
    qkv_sum = over_slots([dot(norm_one_all[slot], qkv_grad[slot], ((0,), (0,))) for slot in each])

    attention_total = reduce_groups([qkv_sum, out_sum])
    attention_total, *hidden_late = lax.optimization_barrier((attention_total, *hidden))

    layer_out, input_grad = [], []
    for slot in each:
        feedforward = scatter_plane(dot(hidden_late[slot], down_w, ((1,), (1,))))
        layer_out.append((middle[slot] + valid_rows[slot] * feedforward).astype(low))
    ffn_sum.hop()
    attention_pieces = swap(attention_total.reshape(contexts, -1, 4 * head_cols), "context")
    for slot in each:
        upstream = norm_one_grad[slot]
        input_grad.append(
            middle_grad[slot] + normalize_back(norm_one[slot], inverse_one[slot], upstream)
        )
    layer_out, input_grad = join_cores(jnp.stack(layer_out)), join_cores(jnp.stack(input_grad))
    layer_out, input_grad, *attention_pieces = ffn_sum.hold((layer_out, input_grad, *attention_pieces))

    ffn_pieces = ffn_sum.finish()

    def column_output(pieces, axis, start, size):
        members, here = lax.axis_size(axis), lax.axis_index(axis)
        whole = jnp.zeros((pieces[0].shape[0], members * size), jnp.float32)
        for step, piece in enumerate(pieces):
            block = piece[:, start : start + size].astype(jnp.float32)
            whole = lax.dynamic_update_slice_in_dim(whole, block, (here ^ step) * size, 1)
        return whole

    def row_output(pieces, axis, start, size):
        members, here = lax.axis_size(axis), lax.axis_index(axis)
        whole = jnp.zeros((members * size, pieces[0].shape[0]), jnp.float32)
        for step, piece in enumerate(pieces):
            block = piece[:, start : start + size].astype(jnp.float32).T
            whole = lax.dynamic_update_slice_in_dim(whole, block, (here ^ step) * size, 0)
        return whole

    grads = tuple(column_output(attention_pieces, "context", i * head_cols, head_cols) for i in range(3)) + (
        row_output(attention_pieces, "context", 3 * head_cols, head_cols),
        column_output(ffn_pieces, "dp", 0, units),
        column_output(ffn_pieces, "dp", units, units),
        row_output(ffn_pieces, "dp", 2 * units, units),
    )
    return (layer_out, input_grad) + grads


def solution(mesh):
    tokens = P("dp", "context", None)
    column = P(("dp", "context"), "tensor")
    row = P("tensor", ("dp", "context"))
    weights = (column, column, column, row, column, column, row)
    return jax.shard_map(
        per_device,
        mesh=mesh,
        in_specs=(tokens, P("dp")) + weights + (tokens,),
        out_specs=(tokens, tokens) + weights,
        check_vma=False,
    )
```

```python
import math

import jax
import jax.numpy as jnp
from jax import lax
from jax.sharding import PartitionSpec as P

HEAD_DIM = 128
SEQUENCE_ROWS = ("context", "tensor")
PLANE_ROWS = ("dp", "tensor")


def rope_tables(positions, head_dim):
    half_dim = head_dim // 2
    inverse_freq = jnp.exp(
        -math.log(10000.0) * jnp.arange(half_dim, dtype=jnp.float32) * 2.0 / head_dim
    )
    angles = positions.astype(jnp.float32)[:, None] * inverse_freq[None, :]
    angles = jnp.concatenate([angles, angles], axis=-1)
    return (jnp.cos(angles)[:, None, :], jnp.sin(angles)[:, None, :])


def rotate(values, cosine, sine):
    half_dim = values.shape[-1] // 2
    turned = jnp.concatenate([-values[..., half_dim:], values[..., :half_dim]], axis=-1)
    return values * cosine + turned * sine


def unrotate(upstream, cosine, sine):
    half_dim = upstream.shape[-1] // 2
    scaled = upstream * sine
    turned = jnp.concatenate([scaled[..., half_dim:], -scaled[..., :half_dim]], axis=-1)
    return upstream * cosine + turned


def normalize(values):
    centered = values - jnp.mean(values, axis=-1, keepdims=True)
    inverse = lax.rsqrt(jnp.mean(centered * centered, axis=-1, keepdims=True) + 1e-05)
    return (centered * inverse, inverse)


def normalize_back(normed, inverse, upstream):
    mean_grad = jnp.mean(upstream, axis=-1, keepdims=True)
    mean_cross = jnp.mean(upstream * normed, axis=-1, keepdims=True)
    return inverse * (upstream - mean_grad - normed * mean_cross)


def dot(left, right, dims):
    return lax.dot_general(left, right, (dims, ((), ())), preferred_element_type=jnp.float32)


def gather_rows(values, axes):
    return lax.all_gather(values, axes, axis=0, tiled=True)


def scatter_rows(values, axes):
    return lax.psum_scatter(values.astype(jnp.bfloat16), axes, scatter_dimension=0, tiled=True).astype(
        jnp.float32
    )


def join_cores(values):
    cores = lax.axis_size("tensor")
    core, rows = lax.axis_index("tensor"), values.shape[1]
    whole = jnp.concatenate([values] * cores, axis=1)
    for step in range(1, cores):
        route = [(i, (i + step) % cores) for i in range(cores)]
        other = lax.ppermute(values, "tensor", route)
        whole = lax.dynamic_update_slice_in_dim(whole, other, ((core - step) % cores) * rows, 1)
    return whole


def put(buffer, piece, index):
    return lax.dynamic_update_slice_in_dim(buffer, piece[None], index, 0)


def take(buffer, index):
    return lax.dynamic_index_in_dim(buffer, index, 0, keepdims=False)


def trade(weight, axis):
    return exchange(jnp.moveaxis(weight, 1, 0), axis)


def gather_groups(mine):
    group, groups = lax.axis_index("dp"), lax.axis_size("dp")
    whole = jnp.zeros((groups,) + mine.shape, mine.dtype)
    whole = put(whole, mine, group)
    for step in range(1, groups):
        route = [(i, i ^ step) for i in range(groups)]
        whole = put(whole, lax.ppermute(mine, "dp", route), group ^ step)
    return whole.reshape(-1, mine.shape[-1])


def reduce_groups(partials):
    group, groups = lax.axis_index("dp"), lax.axis_size("dp")
    parts = [partial.reshape(groups, -1, partial.shape[1]) for partial in partials]

    def term(index):
        return jnp.concatenate([take(part, index) for part in parts], axis=1)

    total = term(group).astype(jnp.float32)
    for step in range(1, groups):
        route = [(i, i ^ step) for i in range(groups)]
        total = total + lax.ppermute(term(group ^ step), "dp", route).astype(jnp.float32)
    return total.astype(jnp.bfloat16)


def swap(pieces, axis):
    members, here = lax.axis_size(axis), lax.axis_index(axis)
    arrived = [take(pieces, here)]
    for step in range(1, members):
        route = [(i, i ^ step) for i in range(members)]
        arrived.append(lax.ppermute(take(pieces, here ^ step), axis, route))
    return arrived


def exchange(pieces, axis):
    here = lax.axis_index(axis)
    mine = jnp.zeros_like(pieces)
    for step, piece in enumerate(swap(pieces, axis)):
        mine = put(mine, piece, here ^ step)
    return mine


def relay_hops(block):
    n = lax.axis_size("context")
    up, down = [], []
    moving_up = moving_down = block
    for step in range(1, n):
        moving_up = lax.ppermute(moving_up, "context", [(i, i + 1) for i in range(step - 1, n - 1)])
        moving_down = lax.ppermute(moving_down, "context", [(i, i - 1) for i in range(1, n - step + 1)])
        up.append(moving_up)
        down.append(moving_down)
    return up, down


def hold(value, hops, index):
    up, down = hops
    if index < len(up):
        value, up[index], down[index] = lax.optimization_barrier((value, up[index], down[index]))
    return value


def assemble(block, hops):
    n, here = lax.axis_size("context"), lax.axis_index("context")
    up, down = hops
    groups, rows, columns = block.shape
    whole = jnp.zeros((groups, n, rows, columns), block.dtype)
    whole = lax.dynamic_update_slice_in_dim(whole, block[:, None], here, 1)
    for step in range(1, n):
        piece = jnp.where(here >= step, up[step - 1], down[n - step - 1])
        whole = lax.dynamic_update_slice_in_dim(whole, piece[:, None], (here - step) % n, 1)
    return whole.reshape(-1, columns)


def scatter_plane(values):
    low = jnp.bfloat16
    cores, groups = lax.axis_size("tensor"), lax.axis_size("dp")
    core, group = lax.axis_index("tensor"), lax.axis_index("dp")
    width = values.shape[1]
    parts = values.astype(low).reshape(groups, cores, -1, width)

    def of_core(index):
        return lax.dynamic_index_in_dim(parts, index % cores, 1, keepdims=False)

    total = of_core(core).astype(jnp.float32)
    for step in range(1, cores):
        route = [(i, (i + step) % cores) for i in range(cores)]
        total = total + lax.ppermute(of_core(core + step), "tensor", route).astype(jnp.float32)
    total = total.astype(low)
    bits = list(range(groups.bit_length() - 1))
    results = []
    for part, order in enumerate((bits, bits[::-1])):
        half = width // 2
        block = total[:, :, part * half : (part + 1) * half]
        rows = block.shape[1]
        block = block.reshape((2,) * len(bits) + (rows, half))
        left = bits[::-1]
        for bit in order:
            axis, mine = left.index(bit), (group >> bit) & 1
            keep = lax.dynamic_index_in_dim(block, mine, axis, keepdims=False)
            send = lax.dynamic_index_in_dim(block, 1 - mine, axis, keepdims=False)
            route = [(i, i ^ (1 << bit)) for i in range(groups)]
            other = lax.ppermute(send, "dp", route)
            block = keep.astype(jnp.float32) + other.astype(jnp.float32)
            left.remove(bit)
            if left:
                block = block.astype(low)
        results.append(block)
    return jnp.concatenate(results, axis=1)


class Reduction:
    def __init__(self, partials, groups, contexts):
        self.parts = [partial.reshape(groups, contexts, -1, partial.shape[1]) for partial in partials]
        self.n, self.here = contexts, lax.axis_index("context")
        self.above = self.below = None
        self.step = 0

    def term(self, index):
        picked = [lax.dynamic_index_in_dim(part, index % self.n, 1, keepdims=False) for part in self.parts]
        return jnp.concatenate(picked, axis=-1).astype(jnp.float32)

    def hop(self):
        if self.step == self.n - 1:
            return
        self.step += 1
        step, n = self.step, self.n
        above, below = self.term(self.here - step), self.term(self.here + step)
        if self.above is not None:
            above, below = above + self.above.astype(jnp.float32), below + self.below.astype(jnp.float32)
        self.above = lax.ppermute(
            above.astype(jnp.bfloat16), "context", [(i, i + 1) for i in range(min(step, n - 1))]
        )
        self.below = lax.ppermute(
            below.astype(jnp.bfloat16), "context", [(i, i - 1) for i in range(max(1, n - step), n)]
        )

    def hold(self, value):
        value, self.above, self.below = lax.optimization_barrier((value, self.above, self.below))
        return value

    def finish(self):
        while self.step < self.n - 1:
            self.hop()
        total = self.term(self.here) + self.above.astype(jnp.float32) + self.below.astype(jnp.float32)
        return swap(total.astype(jnp.bfloat16), "dp")


def per_device(tokens, lengths, w_query, w_key, w_value, w_out, w_gate, w_up, w_down, cotangent):
    low = jnp.bfloat16
    slots, chip_rows, width = tokens.shape
    contexts, cores = lax.axis_size("context"), lax.axis_size("tensor")
    rows = chip_rows // cores
    seq = chip_rows * contexts
    head_cols = w_query.shape[1] // contexts
    groups = lax.axis_size("dp")
    units = w_gate.shape[1] // groups
    heads = head_cols // HEAD_DIM
    scale = 1.0 / math.sqrt(HEAD_DIM)
    core = lax.axis_index("tensor")
    own_start = lax.axis_index("context") * chip_rows + core * rows
    own_positions = own_start + jnp.arange(rows, dtype=jnp.int32)
    positions = jnp.arange(seq, dtype=jnp.int32)
    rope_cos, rope_sin = rope_tables(positions, HEAD_DIM)
    causal = positions[None, :] <= positions[:, None]

    def by_context(weight):
        return weight.reshape(weight.shape[0], contexts, -1)

    attention_part = trade(
        jnp.concatenate([by_context(w) for w in (w_query, w_key, w_value, w_out.T)], axis=2), "context"
    )

    def by_group(weight):
        return jnp.moveaxis(weight.reshape(weight.shape[0], groups, -1), 1, 0)

    ffn_block = exchange(
        jnp.concatenate([by_group(w) for w in (w_gate, w_up, w_down.T)], axis=2), "dp"
    )

    def einsum(form, left, right):
        return jnp.einsum(form, left, right, preferred_element_type=jnp.float32)

    def split(values):
        return values.reshape(seq, heads, HEAD_DIM)

    def own(array, slot):
        return lax.dynamic_slice_in_dim(array[slot], core * rows, rows, 0).astype(jnp.float32)

    each = range(slots)
    own_tokens = [own(tokens, slot) for slot in each]
    valid_rows = [(own_positions < lengths[slot]).astype(jnp.float32)[:, None] for slot in each]
    allowed = [(causal & (positions < lengths[slot])[None, :])[None] for slot in each]
    out_grad = [own(cotangent, slot) * valid_rows[slot] for slot in each]
    ffn_grad = [(valid_rows[slot] * out_grad[slot]).astype(low) for slot in each]
    norm_one, inverse_one = zip(*[normalize(own_tokens[slot]) for slot in each])
    norm_one_all = [gather_rows(norm_one[slot].astype(low), SEQUENCE_ROWS) for slot in each]

    attention_part, ffn_block, *ffn_grad = lax.optimization_barrier(
        (attention_part, ffn_block, *ffn_grad)
    )
    attention_w = gather_groups(attention_part)
    qkv_w, out_w = attention_w[:, : 3 * head_cols], attention_w[:, 3 * head_cols :]
    hops = relay_hops(ffn_block)
    last = slots - 1
    ffn_grad_all = [gather_rows(ffn_grad[slot], PLANE_ROWS) for slot in each]

    def attend(slot):
        qkv = dot(norm_one_all[slot], qkv_w, ((1,), (0,)))
        if slot + 1 < slots:
            qkv, norm_one_all[slot + 1] = lax.optimization_barrier((qkv, norm_one_all[slot + 1]))
        if slot + 1 == last:
            norm_one_all[last] = hold(norm_one_all[last], hops, 0)
        query, key, value = (qkv[:, i * head_cols : (i + 1) * head_cols] for i in range(3))
        query = rotate(split(query), rope_cos, rope_sin).astype(low)
        key = rotate(split(key), rope_cos, rope_sin).astype(low)
        value = split(value.astype(low))
        scores = einsum("qhd,khd->hqk", query, key) * scale
        masked = jnp.where(allowed[slot], scores, -1e30)
        row_top = jnp.max(masked, axis=-1, keepdims=True)
        exponent = jnp.where(allowed[slot], jnp.exp(masked - row_top), 0.0)
        probabilities = exponent / jnp.sum(exponent, axis=-1, keepdims=True)
        attended = einsum("hqk,khd->qhd", probabilities.astype(low), value)
        attended = attended.reshape(seq, heads * HEAD_DIM).astype(low)
        return query, key, value, probabilities, attended

    saved = [attend(slot) for slot in each]
    attended = [kept[4] for kept in saved]
    branch = []
    for slot in each:
        if slot == last:
            attended[slot], *ffn_grad_all = lax.optimization_barrier((attended[slot], *ffn_grad_all))
        part = dot(attended[slot], out_w, ((1,), (1,))).astype(low)
        if slot + 1 < slots:
            part, attended[slot + 1] = lax.optimization_barrier((part, attended[slot + 1]))
        if slot == 0:
            part = hold(part, hops, 1)
        branch.append(scatter_rows(part, SEQUENCE_ROWS) if slot == 0 else part)
    middle, norm_two, inverse_two, norm_two_all = [], [], [], []
    for slot in each:
        summed_branch = branch[slot]
        if slot == 0:
            summed_branch = hold(summed_branch, hops, 2)
        middle.append(own_tokens[slot] + valid_rows[slot] * summed_branch)
        normed, inverse = normalize(middle[slot])
        norm_two.append(normed)
        inverse_two.append(inverse)
        normed = normed.astype(low)
        if slot + 1 < slots:
            normed, part = lax.optimization_barrier((normed, branch[slot + 1]))
        norm_two_all.append(gather_rows(normed, PLANE_ROWS))
        if slot + 1 < slots:
            branch[slot + 1] = scatter_rows(part, SEQUENCE_ROWS)
    ffn_w = assemble(ffn_block, hops)
    gate_up_w, down_w = ffn_w[:, : 2 * units], ffn_w[:, 2 * units :]

    hidden, gate_up_grad, norm_two_grad = [], [], []
    for slot in each:
        gate_up = dot(norm_two_all[slot], gate_up_w, ((1,), (0,)))
        gate, upper = gate_up[:, :units], gate_up[:, units:]
        sigmoid = jax.nn.sigmoid(gate)
        silu = gate * sigmoid
        hidden.append((silu * upper).astype(low))
        hidden_grad = dot(ffn_grad_all[slot], down_w, ((1,), (0,)))
        gate_grad = (hidden_grad * upper * sigmoid * (1.0 + gate * (1.0 - sigmoid))).astype(low)
        upper_grad = (hidden_grad * silu).astype(low)
        gate_up_grad.append(jnp.concatenate([gate_grad, upper_grad], axis=1))
        norm_two_grad.append(dot(gate_up_grad[slot], gate_up_w, ((1,), (1,))).astype(low))

    def over_slots(terms):
        total = terms[0]
        for other in terms[1:]:
            total = total + other
        return total.astype(low)

    down_sum = over_slots([dot(ffn_grad_all[slot], hidden[slot], ((0,), (0,))) for slot in each])
    gate_up_sum = over_slots([dot(norm_two_all[slot], gate_up_grad[slot], ((0,), (0,))) for slot in each])
    norm_two_grad[last], gate_up_sum, down_sum = lax.optimization_barrier(
        (norm_two_grad[last], gate_up_sum, down_sum)
    )
    norm_two_grad = [scatter_plane(norm_two_grad[slot]) for slot in each]
    ffn_sum = Reduction([gate_up_sum, down_sum], groups, contexts)

    middle_grad, branch_grad_all = [], []
    for slot in each:
        upstream = norm_two_grad[slot]
        middle_grad.append(
            out_grad[slot] + normalize_back(norm_two[slot], inverse_two[slot], upstream)
        )
        branch_grad_all.append(
            gather_rows((valid_rows[slot] * middle_grad[slot]).astype(low), SEQUENCE_ROWS)
        )
    ffn_sum.hop()

    qkv_grad, norm_one_grad = [], []
    for slot in each:
        query, key, value, probabilities, _ = saved[slot]
        attended_grad = dot(branch_grad_all[slot], out_w, ((1,), (0,))).astype(low)
        attended_grad = split(attended_grad)
        prob_grad = einsum("qhd,khd->hqk", attended_grad, value)
        row_delta = jnp.sum(probabilities * prob_grad, axis=-1, keepdims=True)
        score_grad = (probabilities * (prob_grad - row_delta)).astype(low)
        query_grad = einsum("hqk,khd->qhd", score_grad, key) * scale
        key_grad = einsum("hqk,qhd->khd", score_grad, query) * scale
        value_grad = einsum("hqk,qhd->khd", probabilities.astype(low), attended_grad)
        qkv_grad.append(
            jnp.concatenate(
                [
                    unrotate(query_grad, rope_cos, rope_sin).astype(low).reshape(seq, -1),
                    unrotate(key_grad, rope_cos, rope_sin).astype(low).reshape(seq, -1),
                    value_grad.astype(low).reshape(seq, -1),
                ],
                axis=1,
            )
        )
        part = dot(qkv_grad[slot], qkv_w, ((1,), (1,))).astype(low)
        if slot + 1 == last:
            part = ffn_sum.hold(part)
        if slot + 1 < slots:
            part, branch_grad_all[slot + 1] = lax.optimization_barrier((part, branch_grad_all[slot + 1]))
        if slot + 1 == last:
            branch_grad_all[last], *hidden_late = lax.optimization_barrier(
                (branch_grad_all[last], *hidden)
            )
        norm_one_grad.append(scatter_rows(part, SEQUENCE_ROWS))
    out_sum = over_slots([dot(branch_grad_all[slot], attended[slot], ((0,), (0,))) for slot in each])
    qkv_sum = over_slots([dot(norm_one_all[slot], qkv_grad[slot], ((0,), (0,))) for slot in each])

    ffn_sum.hop()
    qkv_sum, norm_one_grad[0] = lax.optimization_barrier((qkv_sum, norm_one_grad[0]))
    qkv_sum = ffn_sum.hold(qkv_sum)

    layer_out, input_grad = [], []
    for slot in each:
        feedforward = scatter_plane(dot(hidden_late[slot], down_w, ((1,), (1,))))
        layer_out.append((middle[slot] + valid_rows[slot] * feedforward).astype(low))
    ffn_sum.hop()
    norm_one_grad[0], *layer_out = lax.optimization_barrier((norm_one_grad[0], *layer_out))
    attention_total = ffn_sum.hold(reduce_groups([qkv_sum, out_sum]))
    for slot in each:
        upstream = norm_one_grad[slot]
        input_grad.append(
            middle_grad[slot] + normalize_back(norm_one[slot], inverse_one[slot], upstream)
        )
    layer_out, input_grad = join_cores(jnp.stack(layer_out)), join_cores(jnp.stack(input_grad))

    ffn_pieces = ffn_sum.finish()
    attention_pieces = swap(attention_total.reshape(contexts, -1, 4 * head_cols), "context")

    def column_output(pieces, axis, start, size):
        members, here = lax.axis_size(axis), lax.axis_index(axis)
        whole = jnp.zeros((pieces[0].shape[0], members * size), jnp.float32)
        for step, piece in enumerate(pieces):
            block = piece[:, start : start + size].astype(jnp.float32)
            whole = lax.dynamic_update_slice_in_dim(whole, block, (here ^ step) * size, 1)
        return whole

    def row_output(pieces, axis, start, size):
        members, here = lax.axis_size(axis), lax.axis_index(axis)
        whole = jnp.zeros((members * size, pieces[0].shape[0]), jnp.float32)
        for step, piece in enumerate(pieces):
            block = piece[:, start : start + size].astype(jnp.float32).T
            whole = lax.dynamic_update_slice_in_dim(whole, block, (here ^ step) * size, 0)
        return whole

    grads = tuple(column_output(attention_pieces, "context", i * head_cols, head_cols) for i in range(3)) + (
        row_output(attention_pieces, "context", 3 * head_cols, head_cols),
        column_output(ffn_pieces, "dp", 0, units),
        column_output(ffn_pieces, "dp", units, units),
        row_output(ffn_pieces, "dp", 2 * units, units),
    )
    return (layer_out, input_grad) + grads


def solution(mesh):
    tokens = P("dp", "context", None)
    column = P(("dp", "context"), "tensor")
    row = P("tensor", ("dp", "context"))
    weights = (column, column, column, row, column, column, row)
    return jax.shard_map(
        per_device,
        mesh=mesh,
        in_specs=(tokens, P("dp")) + weights + (tokens,),
        out_specs=(tokens, tokens) + weights,
        check_vma=False,
    )
```
